32 devices in a mesh: dp: 16 (over z, y, core), fsdp: 2 (over x).
Axes of the slice: x: 2, y: 2, z: 4, core: 2. Of those that a mesh axis runs over, the one named last changes fastest.
Arguments:
- tokens: bfloat16 [64, 280, 768], P(('dp', 'fsdp')), may hold values from -6 to 6
- patch_counts: int32 [64], P(('dp', 'fsdp')), may hold values from 100 to 240, as said below
- cotangent: bfloat16 [64, 280, 768], P(('dp', 'fsdp')), may hold values from -6 to 6
- norm1_gain: bfloat16 [768], P('fsdp'), may hold values from 0.5 to 1.5
- norm1_bias: bfloat16 [768], P('fsdp'), may hold values from -1.796875 to 1.796875
- qkv_weight: bfloat16 [768, 2304], P('fsdp'), may hold values from -0.21875 to 0.21875
- qv_bias: bfloat16 [1536], P('fsdp'), may hold values from -1.796875 to 1.796875
- out_weight: bfloat16 [768, 768], P('fsdp'), may hold values from -0.875 to 0.875
- out_bias: bfloat16 [768], P('fsdp'), may hold values from -1.796875 to 1.796875
- norm2_gain: bfloat16 [768], P('fsdp'), may hold values from 0.5 to 1.5
- norm2_bias: bfloat16 [768], P('fsdp'), may hold values from -1.796875 to 1.796875
- up_weight: bfloat16 [768, 3072], P('fsdp'), may hold values from -0.21875 to 0.21875
- up_bias: bfloat16 [3072], P('fsdp'), may hold values from -1.796875 to 1.796875
- down_weight: bfloat16 [3072, 768], P('fsdp'), may hold values from -0.109375 to 0.109375
- down_bias: bfloat16 [768], P('fsdp'), may hold values from -1.796875 to 1.796875
Outputs:
- result: bfloat16 [64, 280, 768], P(('dp', 'fsdp'))
- grad_tokens: bfloat16 [64, 280, 768], P(('dp', 'fsdp'))
- grad_norm1_gain: float32 [768], P('fsdp')
- grad_norm1_bias: float32 [768], P('fsdp')
- grad_qkv_weight: float32 [768, 2304], P('fsdp')
- grad_qv_bias: float32 [1536], P('fsdp')
- grad_out_weight: float32 [768, 768], P('fsdp')
- grad_out_bias: float32 [768], P('fsdp')
- grad_norm2_gain: float32 [768], P('fsdp')
- grad_norm2_bias: float32 [768], P('fsdp')
- grad_up_weight: float32 [768, 3072], P('fsdp')
- grad_up_bias: float32 [3072], P('fsdp')
- grad_down_weight: float32 [3072, 768], P('fsdp')
- grad_down_bias: float32 [768], P('fsdp')
The draws below stay inside these ranges and needn't reach their ends.
Inputs may be any that keep to these rules, and one draw needn't show every extreme that they name: `patch_counts`: patches of each pair; some pair has exactly 240 and some exactly 100.
All inputs are finite; a program needn't handle non-finite values.
Results may differ from the reference program's by a relative error of at most 0.014.
Values may be sent and summed in bfloat16 or wider, within the bound.
A program may use at most 192 MiB of HBM per device.

```python
import math
import jax
import jax.numpy as jnp
from jax import lax

D = 768
FF = 3072
HEAD_DIM = 64
TEXT = 40
PATCH_MIN = 100
PATCH_MAX = 240
LENGTH = 280
PAIRS = 64


def draw_patch_counts(key, part):
    counts = jax.random.randint(key, (PAIRS,), PATCH_MIN, PATCH_MAX + 1, dtype=jnp.int32)
    counts = counts.at[0].set(PATCH_MAX)
    return counts.at[PAIRS - 1].set(PATCH_MIN)


def spiked(entries, rng, source, target, blocks, factor):
    owner, partner = [(jnp.arange(entries.shape[axis_at]) // (entries.shape[axis_at] // blocks)).reshape([-1 if axis == axis_at else 1 for axis in range(entries.ndim)]) for axis_at in (source, target)]
    chosen = jax.random.permutation(rng, blocks)[partner]
    strong = (owner == chosen) | (owner == (partner + blocks // 2) % blocks)
    return jnp.where(strong, factor * entries, entries)


def shard_levels(key, shape, cuts, low, largest):
    factor_of, own = 1.0, jax.random.fold_in(key, 6)
    for dim, shards_of in cuts:
        steps = jnp.exp(jax.random.uniform(jax.random.fold_in(own, dim), (shards_of,), jnp.float32, low / len(cuts), largest / len(cuts)))
        factor_of = factor_of * jnp.repeat(steps, shape[dim] // shards_of).reshape([-1 if axis == dim else 1 for axis in range(len(shape))])
    return factor_of


def normal_values(own_key, dims, spread, reach, shards=(), kind=jnp.bfloat16):
    entries = jax.random.normal(own_key, dims, jnp.float32) * spread
    if len(shards) > 0:
        entries = shard_levels(own_key, dims, shards, -0.22, 0.18) * entries
    return jnp.clip(entries, min=-reach, max=reach).astype(kind)


def heavy_noise(stream_key, shape, scale, limit, shards, heavy, kind=jnp.bfloat16):
    result = scale * jax.random.normal(stream_key, shape, jnp.float32)
    if shards:
        result = result * shard_levels(stream_key, shape, shards, -0.22, 0.18)
    return jnp.clip(spiked(result, jax.random.fold_in(stream_key, 3), *heavy), -limit, limit).astype(kind)


def setup_inputs(seed: int = 0) -> dict:
    seeds = jax.random.split(jax.random.key(seed), 16)
    tokens = normal_values(seeds[0], (PAIRS, LENGTH, D), 1.0, 6.0, ((0, 32),))
    patch_counts = draw_patch_counts(jax.random.fold_in(seeds[15], 71), 0)
    cotangent = heavy_noise(seeds[2], (PAIRS, LENGTH, D), 1.0, 6.0, ((0, 32),), (0, 2, 32, 2.75))
    norm1_gain = jnp.clip(1.0 + 0.1 * jax.random.normal(seeds[3], (D,), jnp.float32), 0.5, 1.5).astype(jnp.bfloat16)
    norm1_bias = normal_values(seeds[4], (D,), 0.3, 1.796875, ((0, 2),))
    qkv_weight = normal_values(seeds[5], (D, 3 * D), D ** -0.5, 0.21875, ((0, 2),))
    qv_bias = normal_values(seeds[6], (2 * D,), 0.3, 1.796875, ((0, 2),))
    out_weight = normal_values(seeds[7], (D, D), (D // 16) ** -0.5, 0.875, ((0, 2),))
    out_bias = normal_values(seeds[8], (D,), 0.3, 1.796875, ((0, 2),))
    norm2_gain = jnp.clip(1.0 + 0.1 * jax.random.normal(seeds[9], (D,), jnp.float32), 0.5, 1.5).astype(jnp.bfloat16)
    norm2_bias = normal_values(seeds[10], (D,), 0.3, 1.796875, ((0, 2),))
    up_weight = normal_values(seeds[11], (D, FF), D ** -0.5, 0.21875, ((0, 2),))
    up_bias = normal_values(seeds[12], (FF,), 0.3, 1.796875, ((0, 2),))
    down_weight = normal_values(seeds[13], (FF, D), FF ** -0.5, 0.109375, ((0, 2),))
    down_bias = normal_values(seeds[14], (D,), 0.3, 1.796875, ((0, 2),))
    return {"tokens": tokens, "patch_counts": patch_counts, "cotangent": cotangent, "norm1_gain": norm1_gain, "norm1_bias": norm1_bias, "qkv_weight": qkv_weight, "qv_bias": qv_bias, "out_weight": out_weight, "out_bias": out_bias, "norm2_gain": norm2_gain, "norm2_bias": norm2_bias, "up_weight": up_weight, "up_bias": up_bias, "down_weight": down_weight, "down_bias": down_bias}


norm_eps = 1e-06

@jax.custom_vjp
def low(v):
    return lax.optimization_barrier(v.astype(jnp.bfloat16)).astype(jnp.float32)

@jax.custom_vjp
def low_back(v):
    return v

def low_keep(v):
    return (low(v), None)

def low_pass(kept, grad):
    return (grad,)

def back_keep(v):
    return (v, None)

def back_low(kept, grad):
    return (low(grad),)
low.defvjp(low_keep, low_pass)
low_back.defvjp(back_keep, back_low)

def normalize(values, gain, shift):
    centered = values - lax.optimization_barrier(jnp.mean(values, axis=-1, keepdims=True))
    variance = lax.optimization_barrier(jnp.mean(centered * centered, axis=-1, keepdims=True))
    return centered * lax.rsqrt(variance + norm_eps) * gain + shift

def block_forward(tokens_block, counts_block, params):
    gain_one, shift_one, qkv_weight, qv_bias, out_weight, out_bias, gain_two, shift_two, up_weight, up_bias, down_weight, down_bias = params
    group, length, width = tokens_block.shape
    heads = width // HEAD_DIM
    highest = lax.Precision.HIGHEST
    normed_one = low(normalize(tokens_block, gain_one, shift_one))
    bias_full = jnp.concatenate([qv_bias[:width], jnp.zeros((width,), jnp.float32), qv_bias[width:]])
    packed = jnp.einsum('gld,de->gle', normed_one, qkv_weight, precision=highest) + bias_full
    packed = low(low_back(packed)).reshape(group, length, 3, heads, HEAD_DIM)
    query = packed[:, :, 0]
    keys = packed[:, :, 1]
    values_all = packed[:, :, 2]
    scores = low_back(jnp.einsum('glhd,gmhd->ghlm', query, keys, precision=highest) * 0.125)
    valid = jnp.arange(length, dtype=jnp.int32)[None, :] < (TEXT + counts_block)[:, None]
    scores = jnp.where(valid[:, None, None, :], scores, -1e+30)
    peak = lax.optimization_barrier(jnp.max(scores, axis=-1, keepdims=True))
    expon = jnp.exp(scores - peak)
    probs = expon / lax.optimization_barrier(jnp.sum(expon, axis=-1, keepdims=True))
    attended = jnp.einsum('ghlm,gmhd->glhd', low(probs), values_all, precision=highest)
    attended = low(low_back(attended)).reshape(group, length, width)
    branch = low_back(jnp.einsum('gld,de->gle', attended, out_weight, precision=highest) + out_bias)
    middle = tokens_block + branch
    normed_two = low(normalize(middle, gain_two, shift_two))
    hidden = low_back(jnp.einsum('gld,df->glf', normed_two, up_weight, precision=highest) + up_bias)
    active = low(jax.nn.gelu(hidden, approximate=False))
    return middle + jnp.einsum('glf,fd->gld', active, down_weight, precision=highest) + down_bias

def reference(tokens, patch_counts, cotangent, norm1_gain, norm1_bias, qkv_weight, qv_bias, out_weight, out_bias, norm2_gain, norm2_bias, up_weight, up_bias, down_weight, down_bias):
    params = tuple((piece.astype(jnp.float32) for piece in (norm1_gain, norm1_bias, qkv_weight, qv_bias, out_weight, out_bias, norm2_gain, norm2_bias, up_weight, up_bias, down_weight, down_bias)))
    pairs, length, width = tokens.shape
    group = math.gcd(pairs, 16)
    count_groups = pairs // group

    def forward(tokens_f, params_f):

        def step(carry, item):
            tokens_block, counts_block = item
            return (carry, block_forward(tokens_block, counts_block, params_f))
        _, outputs = lax.scan(jax.checkpoint(step), jnp.zeros((), jnp.float32), (tokens_f.reshape(count_groups, group, length, width), patch_counts.reshape(count_groups, group)))
        return outputs.reshape(pairs, length, width)
    output, pullback = jax.vjp(forward, tokens.astype(jnp.float32), params)
    grad_input, grad_params = pullback(cotangent.astype(jnp.float32))
    return (output.astype(jnp.bfloat16), grad_input.astype(jnp.bfloat16), grad_params[0], grad_params[1], grad_params[2], grad_params[3], grad_params[4], grad_params[5], grad_params[6], grad_params[7], grad_params[8], grad_params[9], grad_params[10], grad_params[11])
```

```python
import functools

import jax
import jax.numpy as jnp
from jax import lax
from jax.experimental import pallas as pl
from jax.experimental.pallas import tpu as pltpu
from jax.sharding import PartitionSpec as P

TEXT = 40
MESH = pl.DeviceIdType.MESH
BF16 = jnp.bfloat16
F32 = jnp.float32
EPS = 1e-06
NZ = 4
GROUP = 16
PAIRS = 2
LENGTH = 280
LPAD = 288
ROWS = PAIRS * LPAD
D = 768
FF = 3072
HALF = D // 2
NCH = 18
WINDOW = 3
PIECES = (
    [(0, 32 * j, 32) for j in range(3)]
    + [(1, 0, 96)]
    + [(2, 32 * j, 32) for j in range(3)]
    + [(3, 96 * j, 96) for j in range(4)]
)
SMALL = (1, 1, 2, 1, 1, 1, 4, 1)
G1, B1, QV, OB, G2, B2, UB, DB = 0, 1, 2, 4, 5, 6, 7, 11
CHAINED = tuple(range(10)) + (13, 14)


def dot(a, b):
    return jnp.dot(a, b, preferred_element_type=F32)


def dot_nt(a, b):
    return lax.dot_general(a, b, (((1,), (1,)), ((), ())), preferred_element_type=F32)


def dot_tn(a, b):
    return lax.dot_general(a, b, (((0,), (0,)), ((), ())), preferred_element_type=F32)


def mult(x, n):
    return x if isinstance(x, int) else pl.multiple_of(x, n)


def ds(start, size, n=None):
    return pl.ds(mult(start, n or size), size)


def places():
    d = lax.axis_index("dp")
    f = lax.axis_index("fsdp")
    core = lax.rem(d, 2)
    y = lax.rem(d // 2, 2)
    z = lax.rem(d // 4, NZ)
    base = d - lax.rem(d, GROUP)

    def at(zz, yy, cc):
        return base + zz * 4 + yy * 2 + cc

    peers = {
        "c": (at(z, y, 1 - core), f),
        "x": (d, 1 - f),
        "y": (at(z, 1 - y, core), f),
    }
    for k in range(1, NZ):
        peers["z%d" % k] = (at(lax.rem(z + k, NZ), y, core), f)
    return f, core, y, z, peers


def norm_parts(v):
    c = v - jnp.mean(v, axis=-1, keepdims=True)
    r = lax.rsqrt(jnp.mean(c * c, axis=-1, keepdims=True) + EPS)
    return c * r, r


def layer_kernel(
    counts, tok, cot, w0, w1, w2, w3, s_in,
    res, gtok, gdown, gup, gqo, gsmall,
    xs, dys, h, lt, qkv, o, lse, x1, gact, dact, dh, vec, smv,
    v0, v1, v2, v3,
    own, snd, ownd, sndd,
    cb, xb, yb, zb, stg, cbd, xbd, ybd, zbd, stgd, sacc, srecv,
    gxs, gys, gcs, lsem, csem, xsem, ysem, zsem, azsem, aysem, acsem, psem, ssem,
):
    f, core, y, z, peers = places()
    ins = (w0, w1, w2, w3)
    ws = (v0, v1, v2, v3)
    barrier = pltpu.get_barrier_semaphore()
    for name in peers:
        pl.semaphore_signal(barrier, inc=1, device_id=peers[name], device_id_type=MESH)

    def send(src, dst, sems, idx, name):
        return pltpu.make_async_remote_copy(
            src_ref=src, dst_ref=dst, send_sem=sems.at[(0,) + idx], recv_sem=sems.at[(1,) + idx],
            device_id=peers[name], device_id_type=MESH,
        )

    def piece(g, half, yy):
        w, r0, rows = PIECES[g]
        full = ins[w].shape[0]
        return w, pl.ds(pl.multiple_of(half * full + (core * 2 + yy) * (full // 4) + r0, 16), rows)

    def gx(g):
        w, there = piece(g, f, y)
        _, here = piece(g, 0, y)
        return send(ins[w].at[here], ws[w].at[there], gxs, (g,), "x")

    def gy(g):
        w, at = piece(g, 1 - f, y)
        return send(ws[w].at[at], ws[w].at[at], gys, (g,), "y")

    def gc(g, k):
        w, at = piece(g, 1 - f, y if k == 0 else 1 - y)
        return send(ws[w].at[at], ws[w].at[at], gcs, (g, k), "c")

    def got_x(g):
        gx(g).wait()
        if g + WINDOW < len(PIECES):
            gx(g + WINDOW).start()
        gy(g).start()
        gc(g, 0).start()

    def got_y(g):
        gy(g).wait()
        gc(g, 1).start()

    def got(g):
        gc(g, 0).wait()
        gc(g, 1).wait()

    local = []
    for i in range(4):
        full = ins[i].shape[0]
        local.append(pltpu.make_async_copy(ins[i], ws[i].at[pl.ds(pl.multiple_of(f * full, 16), full)], lsem.at[i]))
    local.append(pltpu.make_async_copy(s_in, smv.at[f], lsem.at[4]))
    for cp in local:
        cp.start()
    pl.semaphore_wait(barrier, len(peers))
    small_x = send(s_in, smv.at[f], ssem, (6,), "x")
    small_x.start()
    for g in range(WINDOW):
        gx(g).start()

    def c_copy(i, down):
        if down:
            return send(sndd.at[lax.rem(i, 2)], cbd.at[i], csem, (i,), "c")
        return send(snd.at[lax.rem(i, 2)], cb.at[i - 6], csem, (i,), "c")

    def x_copy(i):
        if i < 6:
            return send(cbd.at[i, 1 - f], xbd.at[i], xsem, (i,), "x")
        return send(cb.at[i - 6, 1 - f], xb.at[i - 6], xsem, (i,), "x")

    def bufs(i):
        if i < 6:
            return i, 128, D, cbd, xbd, ybd, zbd, stgd
        return i - 6, HALF, 256, cb, xb, yb, zb, stg

    def y_copy(i):
        j, ur, uc, _, xx, yy, _, _ = bufs(i)
        return send(xx.at[j, ds((1 - y) * (ur // 2), ur // 2)], yy.at[j], ysem, (i,), "y")

    def z_copy(i, k):
        j, ur, uc, _, _, yy, zz, _ = bufs(i)
        return send(
            yy.at[j, ds(lax.rem(z + k, NZ) * (ur // 8), ur // 8)], zz.at[j, k - 1], zsem, (i, k - 1), "z%d" % k
        )

    def outpart(i, start, rows):
        j = i % 6 if i < 12 else (i - 12 + 5) % 6
        if i < 6:
            return gdown.at[pl.ds(pl.multiple_of((2 * j + core) * 128 + start, 16), rows), :]
        ref = gup if i < 12 else gqo
        return ref.at[pl.ds(mult(start, 16), rows), ds((2 * j + core) * 256, 256)]

    def own_piece(i):
        j, ur, uc, _, _, _, _, st = bufs(i)
        return outpart(i, y * (ur // 2) + z * (ur // 8), ur // 8), st.at[j]

    def p_copy(i):
        dst, src = own_piece(i)
        return pltpu.make_async_copy(src, dst, psem.at[i])

    def az_copy(i, k):
        dst, src = own_piece(i)
        return send(src, dst, azsem, (i, k - 1), "z%d" % k)

    def ay_copy(i):
        ur = 128 if i < 6 else HALF
        part = outpart(i, y * (ur // 2), ur // 2)
        return send(part, part, aysem, (i,), "y")

    def ac_copy(i):
        ur = 128 if i < 6 else HALF
        part = outpart(i, 0, ur)
        return send(part, part, acsem, (i,), "c")

    def s1(i, down):
        c_copy(i, down).wait()
        if down:
            cbd[i] = (cbd[i].astype(F32) + ownd[lax.rem(i, 2)].astype(F32)).astype(BF16)
        else:
            cb[i - 6] = (cb[i - 6].astype(F32) + own[lax.rem(i, 2)].astype(F32)).astype(BF16)

    def s2(i):
        x_copy(i).wait()
        if i in CHAINED:
            x_copy(i + WINDOW).start()
        j, ur, uc, cc, xx, _, _, _ = bufs(i)
        xx[j] = (xx[j].astype(F32) + cc[j, f].astype(F32)).astype(BF16)
        y_copy(i).start()

    def s3(i):
        y_copy(i).wait()
        j, ur, uc, _, xx, yy, _, _ = bufs(i)
        yy[j] = (yy[j].astype(F32) + xx[j, ds(y * (ur // 2), ur // 2)].astype(F32)).astype(BF16)
        for k in range(1, NZ):
            z_copy(i, k).start()

    def s4(i):
        for k in range(1, NZ):
            z_copy(i, k).wait()
        j, ur, uc, _, _, yy, zz, st = bufs(i)
        total = yy[j, ds(z * (ur // 8), ur // 8)].astype(F32)
        for k in range(1, NZ):
            total = total + zz[j, k - 1].astype(F32)
        st[j] = total.astype(BF16)
        p_copy(i).start()
        for k in range(1, NZ):
            az_copy(i, k).start()

    def s5(i):
        p_copy(i).wait()
        for k in range(1, NZ):
            az_copy(i, k).wait()
        ay_copy(i).start()

    def s6(i):
        ay_copy(i).wait()
        ac_copy(i).start()

    def s7(i):
        ac_copy(i).wait()

    def slot(k):
        for lag, stage in enumerate((s2, s3, s4, s5, s6, s7)):
            if 0 <= k - lag < NCH:
                stage(k - lag)

    for p in range(PAIRS):
        xs[p * LPAD : p * LPAD + LENGTH] = tok[p].astype(F32)
        xs[p * LPAD + LENGTH : (p + 1) * LPAD] = jnp.zeros((LPAD - LENGTH, D), F32)
        dys[p * LPAD : (p + 1) * LPAD] = jnp.concatenate(
            [cot[p].astype(F32), jnp.zeros((LPAD - LENGTH, D), F32)], axis=0
        ).astype(BF16)

    local[4].wait()
    small_x.wait()
    s0 = smv[0].astype(F32)
    s1v = smv[1].astype(F32)
    for j, r in enumerate((G1, B1, OB, G2, B2, DB)):
        vec[j] = jnp.concatenate([s0[r : r + 1], s1v[r : r + 1]], axis=1)
    vec[6] = jnp.concatenate([s0[QV : QV + 1], s0[QV + 1 : QV + 2]], axis=1)
    vec[7] = jnp.zeros((1, D), F32)
    vec[8] = jnp.concatenate([s1v[QV : QV + 1], s1v[QV + 1 : QV + 2]], axis=1)
    vec[9] = jnp.concatenate([s0[UB : UB + 1], s0[UB + 1 : UB + 2]], axis=1)
    vec[10] = jnp.concatenate([s0[UB + 2 : UB + 3], s0[UB + 3 : UB + 4]], axis=1)
    vec[11] = jnp.concatenate([s1v[UB : UB + 1], s1v[UB + 1 : UB + 2]], axis=1)
    vec[12] = jnp.concatenate([s1v[UB + 2 : UB + 3], s1v[UB + 3 : UB + 4]], axis=1)

    def loop(n, body):
        def step(i, carry):
            body(i)
            return carry

        lax.fori_loop(0, n, step, 0)

    def transpose_into(src, k):
        def body(j):
            cols = ds(j * 128, 128)
            lt[k, cols, :] = src[:, cols].astype(F32).T.astype(BF16)

        loop(D // 128, body)

    def ln1(i):
        rows = ds(i * 96, 96)
        n, _ = norm_parts(xs[rows])
        h[rows] = (n * vec[0] + vec[1]).astype(BF16)

    loop(6, ln1)
    got_x(0)
    transpose_into(h, 0)
    got_x(1)
    got_y(0)
    got_x(2)
    got_y(1)
    got_x(3)
    got_y(2)
    for g in range(3):
        got(g)
    local[0].wait()

    def qkv_body(i):
        cols = ds(i * D, D)
        qkv[:, cols] = (dot(h[...], v0[:, cols]) + vec[6 + i]).astype(BF16)

    loop(3, qkv_body)
    lane = lax.broadcasted_iota(jnp.int32, (1, 128), 1)
    low = lane < 64
    key = lax.broadcasted_iota(jnp.int32, (1, LPAD), 1)

    def attend(i):
        for when, todo in ((1, lambda: (got_x(4), got_y(3))), (4, lambda: (got_x(5), got_y(4))), (7, lambda: (got_x(6), got_y(5))), (10, lambda: (got_x(7), got_y(6)))):
            pl.when(i == when)(lambda todo=todo: (todo(), None)[1])
        p = i // 6
        hp = lax.rem(i, 6)
        rows = ds(p * LPAD, LPAD)
        q = qkv[rows, ds(hp * 128, 128)].astype(F32) * 0.125
        k = qkv[rows, ds(D + hp * 128, 128)]
        v = qkv[rows, ds(2 * D + hp * 128, 128)]
        valid = key < TEXT + counts[p]
        outs = []
        ls = lse[rows]
        for e in range(2):
            qm = jnp.where(low if e == 0 else jnp.logical_not(low), q, 0.0).astype(BF16)
            s = jnp.where(valid, dot_nt(qm, k), -1e30)
            m = jnp.max(s, axis=-1, keepdims=True)
            ex = jnp.exp(s - m)
            t = jnp.sum(ex, axis=-1, keepdims=True)
            ls = jnp.where(lane == 2 * hp + e, m + jnp.log(t), ls)
            outs.append(dot((ex / t).astype(BF16), v))
        lse[rows] = ls
        o[rows, ds(hp * 128, 128)] = jnp.where(low, outs[0], outs[1]).astype(BF16)

    loop(12, attend)
    got(3)
    local[1].wait()

    def proj(i):
        cols = ds(i * 256, 256)
        x1[:, cols] = xs[:, cols] + dot(o[...], v1[:, cols]) + vec[2, :, cols]

    loop(3, proj)
    got_y(7)

    def ln2(i):
        rows = ds(i * 96, 96)
        n, _ = norm_parts(x1[rows])
        h[rows] = (n * vec[3] + vec[4]).astype(BF16)

    loop(6, ln2)
    got_x(8)
    transpose_into(o, 1)
    transpose_into(h, 2)
    for g in range(4, 7):
        got(g)
    local[2].wait()

    def up_tile(j):
        cols = ds(j * 256, 256)
        u = dot(h[...], v2[:, cols]) + vec[9 + j // 3, :, ds(lax.rem(j, 3) * 256, 256)]
        phi = 0.5 * (1.0 + lax.erf(u * 0.7071067811865476))
        gact[:, cols] = (u * phi).astype(BF16)
        dact[:, cols] = (phi + u * (0.3989422804014327 * jnp.exp(-0.5 * u * u))).astype(BF16)

    def down_chunk(i):
        par = lax.rem(i, 2)
        for x in range(2):
            cols = x * (FF // 2) + i * 256
            mine = gact[:, ds(cols + core * 128, 128)]
            other = gact[:, ds(cols + (1 - core) * 128, 128)]
            both = jnp.concatenate([mine, other], axis=1)
            for n in range(3):
                r = dot_tn(both, dys[:, n * 256 : (n + 1) * 256]).astype(BF16)
                ownd[par, x, :, n * 256 : (n + 1) * 256] = r[:128]
                sndd[par, x, :, n * 256 : (n + 1) * 256] = r[128:]
        c_copy(i, True).start()

    def phase_a(i):
        up_tile(i)
        up_tile(6 + i)
        down_chunk(i)

        @pl.when(i > 0)
        def _():
            s1(i - 1, True)

        for when, todo in (
            (0, lambda: (got_x(9), got_y(8))),
            (1, lambda: (got_x(10), got_y(9), x_copy(0).start())),
            (2, lambda: (got_y(10), x_copy(1).start())),
            (3, lambda: x_copy(2).start()),
            (4, lambda: slot(0)),
            (5, lambda: slot(1)),
        ):
            pl.when(i == when)(lambda todo=todo: (todo(), None)[1])

    loop(6, phase_a)
    s1(5, True)
    for g in range(7, 11):
        got(g)
    local[3].wait()

    def down_proj(n):
        cols = ds(n * 256, 256)
        r = (x1[:, cols] + dot(gact[...], v3[:, cols]) + vec[5, :, cols])
        for p in range(PAIRS):
            res[p, :, cols] = r[p * LPAD : p * LPAD + LENGTH].astype(BF16)

    loop(3, down_proj)
    slot(2)

    def du_tile(j):
        cols = ds(j * 256, 256)
        du = (dot_nt(dys[...], v3[cols, :]) * dact[:, cols].astype(F32)).astype(BF16)
        dact[:, cols] = du
        sums = jnp.sum(du.astype(F32), axis=0, keepdims=True)
        for e in range(2):
            sacc[j // 6, 3 * UB + 2 * lax.rem(j, 6) + e] = sums[:, e * 128 : (e + 1) * 128]

    def col_chunk(i, j, sel, src):
        par = lax.rem(i, 2)
        for side, dst in ((core, own), (1 - core, snd)):
            u = 2 * j + side
            col_unit(dst, par, u, sel, src)
        c_copy(i, False).start()

    def col_unit(dst, par, u, sel, src):
        r = dot(lt[sel], src[:, ds(u * 256, 256)]).astype(BF16)
        dst[par, 0] = r[:HALF]
        dst[par, 1] = r[HALF:]

    def phase_c(j):
        du_tile(2 * j)
        du_tile(2 * j + 1)
        col_chunk(6 + j, j, 2, dact)

        @pl.when(j > 0)
        def _():
            s1(5 + j, False)

        for when, todo in ((2, lambda: slot(3)), (5, lambda: slot(4))):
            pl.when(j == when)(lambda todo=todo: (todo(), None)[1])

    loop(6, phase_c)
    s1(11, False)

    def dh2_tile(n):
        cols = ds(n * 256, 256)
        dh[:, cols] = dot_nt(dact[...], v2[cols, :])

    loop(3, dh2_tile)
    slot(5)
    zero = jnp.zeros((1, D), F32)

    def spread(x, r, v):
        for j in range(v.shape[1] // 128):
            sacc[x, 3 * r + j] = v[:, j * 128 : (j + 1) * 128]

    def put(r, v):
        spread(0, r, v[:, :HALF])
        spread(1, r, v[:, HALF:])

    def ln2_back(i, carry):
        a, b, c2, d2 = carry
        rows = ds(i * 96, 96)
        n, r = norm_parts(x1[rows])
        g = dh[rows]
        e = g * vec[3]
        dy = dys[rows].astype(F32)
        dx = dy + r * (
            e - jnp.mean(e, axis=-1, keepdims=True) - n * jnp.mean(e * n, axis=-1, keepdims=True)
        )
        x1[rows] = dx
        da = dx.astype(BF16)
        qkv[rows, 3 * D :] = da
        return (
            a + jnp.sum(g * n, axis=0, keepdims=True),
            b + jnp.sum(g, axis=0, keepdims=True),
            c2 + jnp.sum(da.astype(F32), axis=0, keepdims=True),
            d2 + jnp.sum(dy, axis=0, keepdims=True),
        )

    sums = lax.fori_loop(0, 6, ln2_back, (zero, zero, zero, zero))
    for r, v in zip((G2, B2, OB, DB), sums):
        put(r, v)

    col_chunk(12, 5 + core // 2, 1, qkv)

    def do_tile(n):
        cols = ds(n * 256, 256)
        o[:, cols] = dot_nt(qkv[:, 3 * D :], v1[cols, :]).astype(BF16)

    loop(3, do_tile)
    s1(12, False)
    slot(6)

    def attend_back(i):
        for when, todo in ((2, lambda: slot(7)), (5, lambda: slot(8)), (8, lambda: slot(9)), (11, lambda: slot(10))):
            pl.when(i == when)(lambda todo=todo: (todo(), None)[1])
        p = i // 6
        hp = lax.rem(i, 6)
        rows = ds(p * LPAD, LPAD)
        q = qkv[rows, ds(hp * 128, 128)]
        k = qkv[rows, ds(D + hp * 128, 128)]
        v = qkv[rows, ds(2 * D + hp * 128, 128)]
        g = o[rows, ds(hp * 128, 128)]
        qf = q.astype(F32) * 0.125
        gf = g.astype(F32)
        valid = key < TEXT + counts[p]
        ls = lse[rows]
        got3 = []
        for e in range(2):
            keep = low if e == 0 else jnp.logical_not(low)
            qm = jnp.where(keep, qf, 0.0).astype(BF16)
            gm = jnp.where(keep, gf, 0.0).astype(BF16)
            total = jnp.sum(jnp.where(lane == 2 * hp + e, ls, 0.0), axis=-1, keepdims=True)
            pr = jnp.where(valid, jnp.exp(dot_nt(qm, k) - total), 0.0)
            dp = dot_nt(gm, v)
            dsc = (pr * (dp - jnp.sum(pr * dp, axis=-1, keepdims=True))).astype(BF16)
            got3.append((dot(dsc, k), dot_tn(dsc, q), dot_tn(pr.astype(BF16), g)))
        for part, scale in ((0, 0.125), (1, 0.125), (2, 1.0)):
            r = jnp.where(low, got3[0][part], got3[1][part]) * scale
            qkv[rows, ds(part * D + hp * 128, 128)] = r.astype(BF16)

    loop(12, attend_back)

    def phase_g(t):
        j = t + 1
        col_chunk(12 + j, t, 0, qkv)

        @pl.when(t > 0)
        def _():
            s1(11 + j, False)

        for when, todo in (
            (1, lambda: x_copy(13).start()),
            (2, lambda: (slot(11), x_copy(14).start())),
            (3, lambda: x_copy(15).start()),
        ):
            pl.when(t == when)(lambda todo=todo: (todo(), None)[1])

    loop(4, phase_g)
    for c in range(2):

        @pl.when(core == c)
        def _():
            for side, dst in ((c, own), (1 - c, snd)):
                col_unit(dst, 1, 8 + side, side, qkv)

    c_copy(17, False).start()
    s1(16, False)
    slot(12)
    s1(17, False)

    def dh1_tile(n):
        cols = ds(n * 256, 256)
        dh[:, cols] = dot_nt(qkv[:, : 3 * D], v0[cols, :])

    loop(3, dh1_tile)
    slot(13)

    def ln1_back(i, carry):
        a, b, qs, vs = carry
        rows = ds(i * 96, 96)
        n, r = norm_parts(xs[rows])
        g = dh[rows]
        e = g * vec[0]
        xs[rows] = x1[rows] + r * (
            e - jnp.mean(e, axis=-1, keepdims=True) - n * jnp.mean(e * n, axis=-1, keepdims=True)
        )
        return (
            a + jnp.sum(g * n, axis=0, keepdims=True),
            b + jnp.sum(g, axis=0, keepdims=True),
            qs + jnp.sum(qkv[rows, :D].astype(F32), axis=0, keepdims=True),
            vs + jnp.sum(qkv[rows, 2 * D : 3 * D].astype(F32), axis=0, keepdims=True),
        )

    ga, gb, qs, vs = lax.fori_loop(0, 6, ln1_back, (zero, zero, zero, zero))
    put(G1, ga)
    put(B1, gb)
    for x, v in ((0, qs), (1, vs)):
        spread(x, QV, v)
    for p in range(PAIRS):
        gtok[p] = xs[p * LPAD : p * LPAD + LENGTH].astype(BF16)

    k = 14
    for j, name in enumerate(("c", "x", "y")):
        cp = send(sacc, srecv.at[j], ssem, (j,), name)
        cp.start()
        slot(k)
        k += 1
        cp.wait()
        sacc[...] = sacc[...] + srecv[j]
    copies = [send(sacc, srecv.at[3 + z], ssem, (2 + k2,), "z%d" % k2) for k2 in range(1, NZ)]
    for cp in copies:
        cp.start()
    srecv[3 + z] = sacc[...]
    slot(k)
    k += 1
    for cp in copies:
        cp.wait()
    gsmall[...] = (srecv[3, f] + srecv[4, f]) + (srecv[5, f] + srecv[6, f])
    while k < NCH + 5:
        slot(k)
        k += 1


def layer(*arrays):
    vm = pltpu.VMEM
    dma = pltpu.SemaphoreType.DMA
    any_ = pl.BlockSpec(memory_space=pl.ANY)
    inside = pl.BlockSpec(memory_space=pltpu.VMEM)
    pieces = len(PIECES)
    return pl.pallas_call(
        layer_kernel,
        out_shape=[
            jax.ShapeDtypeStruct((PAIRS, LENGTH, D), BF16),
            jax.ShapeDtypeStruct((PAIRS, LENGTH, D), BF16),
            jax.ShapeDtypeStruct((FF // 2, D), BF16),
            jax.ShapeDtypeStruct((HALF, FF), BF16),
            jax.ShapeDtypeStruct((HALF, FF), BF16),
            jax.ShapeDtypeStruct((36, 1, 128), F32),
        ],
        in_specs=[pl.BlockSpec(memory_space=pltpu.SMEM), inside, inside] + [any_] * 5,
        out_specs=[inside, inside, any_, any_, any_, inside],
        scratch_shapes=[
            vm((ROWS, D), F32),
            vm((ROWS, D), BF16),
            vm((ROWS, D), BF16),
            vm((3, D, ROWS), BF16),
            vm((ROWS, 4 * D), BF16),
            vm((ROWS, D), BF16),
            vm((ROWS, 128), F32),
            vm((ROWS, D), F32),
            vm((ROWS, FF), BF16),
            vm((ROWS, FF), BF16),
            vm((ROWS, D), F32),
            vm((13, 1, D), F32),
            vm((2, 16, HALF), BF16),
            vm((D, 3 * D), BF16),
            vm((D, D), BF16),
            vm((D, FF), BF16),
            vm((FF, D), BF16),
            vm((2, 2, HALF, 256), BF16),
            vm((2, 2, HALF, 256), BF16),
            vm((2, 2, 128, D), BF16),
            vm((2, 2, 128, D), BF16),
            vm((12, 2, HALF, 256), BF16),
            vm((12, HALF, 256), BF16),
            vm((12, HALF // 2, 256), BF16),
            vm((12, NZ - 1, HALF // 8, 256), BF16),
            vm((12, HALF // 8, 256), BF16),
            vm((6, 2, 128, D), BF16),
            vm((6, 128, D), BF16),
            vm((6, 64, D), BF16),
            vm((6, NZ - 1, 16, D), BF16),
            vm((6, 16, D), BF16),
            vm((2, 36, 1, 128), F32),
            vm((7, 2, 36, 1, 128), F32),
            dma((2, pieces)),
            dma((2, pieces)),
            dma((2, pieces, 2)),
            dma((5,)),
            dma((2, NCH)),
            dma((2, NCH)),
            dma((2, NCH)),
            dma((2, NCH, NZ - 1)),
            dma((2, NCH, NZ - 1)),
            dma((2, NCH)),
            dma((2, NCH)),
            dma((NCH,)),
            dma((2, 7)),
        ],
        compiler_params=pltpu.CompilerParams(
            collective_id=1, has_side_effects=True, vmem_limit_bytes=63 << 20
        ),
        name="layer",
    )(*arrays)


def on_device(extra, tokens, patch_counts, cotangent, norm1_gain, norm1_bias, qkv_weight, qv_bias,
              out_weight, out_bias, norm2_gain, norm2_bias, up_weight, up_bias, down_weight, down_bias):
    small = jnp.concatenate(
        [norm1_gain, norm1_bias, qv_bias, out_bias, norm2_gain, norm2_bias, up_bias, down_bias,
         jnp.zeros((4 * HALF,), BF16)]
    ).reshape(16, HALF)
    result, grad_tokens, gdown, gup, gqo, gsmall = layer(
        patch_counts, tokens, cotangent, qkv_weight, out_weight, up_weight, down_weight, small
    )
    grads = [g.astype(F32) for g in (gdown, gup, gqo[:, : 3 * D], gqo[:, 3 * D :])] + [gsmall]
    if extra is not None:
        grads = lax.psum(grads, "dp", axis_index_groups=extra)
    down, up, qkv, out, gsmall = grads
    parts, at = [], 0
    for count in SMALL:
        parts.append(gsmall[3 * at : 3 * (at + count)].reshape(-1))
        at += count
    return (
        result, grad_tokens, parts[0], parts[1], qkv, parts[2], out, parts[3],
        parts[4], parts[5], up, parts[6], down, parts[7],
    )


def solution(mesh):
    dp = mesh.shape["dp"]
    extra = None
    if dp > GROUP:
        extra = [[j + GROUP * i for i in range(dp // GROUP)] for j in range(GROUP)]
    row = P(("dp", "fsdp"), None, None)
    vec = P("fsdp")
    mat = P("fsdp", None)
    return jax.shard_map(
        functools.partial(on_device, extra),
        mesh=mesh,
        in_specs=(row, P(("dp", "fsdp")), row, vec, vec, mat, vec, mat, vec, vec, vec, mat, vec, mat, vec),
        out_specs=(row, row, vec, vec, mat, vec, mat, vec, vec, vec, mat, vec, mat, vec),
        check_vma=False,
    )
```

```python
import functools

import jax
import jax.numpy as jnp
from jax import lax
from jax.experimental import pallas as pl
from jax.experimental.pallas import tpu as pltpu
from jax.sharding import PartitionSpec as P

TEXT = 40
MESH = pl.DeviceIdType.MESH
BF16 = jnp.bfloat16
F32 = jnp.float32
EPS = 1e-06
NZ = 4
GROUP = 16
PAIRS = 2
LENGTH = 280
LPAD = 288
ROWS = PAIRS * LPAD
D = 768
FF = 3072
HALF = D // 2
NCH = 18
GW = 3
PIECES = (
    [(0, 16 * j, 16) for j in range(6)]
    + [(3, 0, 96)]
    + [(1, 48 * j, 48) for j in range(2)]
    + [(2, 16 * j, 16) for j in range(6)]
)
SHARED = 6
GLAG = 3
GATHER_AT = ((9,), (10,), (11,), (12,), (), (13,), (), (14,), (15,), (16,), (17,), ())
SMALL = (1, 1, 2, 1, 1, 1, 4, 1)
G1, B1, QV, OB, G2, B2, UB, DB = 0, 1, 2, 4, 5, 6, 7, 11


def plan():
    points = list(POINTS)
    points += [("Z%d" % n, NCH, n + 1) for n in range(points[-1][2], SLOTS)]
    acts, done, started = {}, 0, 0
    for name, ready, upto in points:
        todo = acts[name] = []
        while True:
            ahead = AHEAD if done < NARROW else AHEAD_LAST
            while started < min(2 * NCH, 2 * ready, done + ahead):
                todo.append(("start", started))
                started += 1
            if done == upto:
                break
            assert done >= 2 * NCH or started > done
            todo.append(("slot", done))
            done += 1
    return acts


POINTS = (
    ("A2", 1, 0), ("A3", 2, 1), ("A4", 3, 2), ("A5", 4, 3), ("B", 6, 5), ("C0", 6, 5), ("C1", 6, 6), ("C2", 7,
    7), ("C3", 8, 8), ("C4", 9, 9), ("C5", 10, 9), ("D", 12, 10), ("E0", 12, 12), ("E", 13, 13), ("F0", 13,
    13), ("F1", 13, 13), ("F2", 13, 14), ("F3", 13, 14), ("F4", 13, 15), ("F5", 13, 15), ("F6", 13, 16),
    ("F7", 13, 17), ("F8", 13, 17), ("F9", 13, 18), ("F10", 13, 18), ("F11", 13, 19), ("G2", 14, 20), ("G3",
    15, 21), ("G4", 16, 22), ("H", 18, 23), ("I", 18, 24),
)
SLOTS = 2 * NCH + 14
AHEAD, AHEAD_LAST, NARROW = 6, 3, 24
PLAN = plan()


def dot(a, b):
    return jnp.dot(a, b, preferred_element_type=F32)


def dot_nt(a, b):
    return lax.dot_general(a, b, (((1,), (1,)), ((), ())), preferred_element_type=F32)


def dot_tn(a, b):
    return lax.dot_general(a, b, (((0,), (0,)), ((), ())), preferred_element_type=F32)


def mult(x, n):
    return x if isinstance(x, int) else pl.multiple_of(x, n)


def ds(start, size, n=None):
    return pl.ds(mult(start, n or size), size)


def places():
    d = lax.axis_index("dp")
    f = lax.axis_index("fsdp")
    core = lax.rem(d, 2)
    y = lax.rem(d // 2, 2)
    z = lax.rem(d // 4, NZ)
    base = d - lax.rem(d, GROUP)

    def at(zz, yy, cc):
        return base + zz * 4 + yy * 2 + cc

    peers = {
        "c": (at(z, y, 1 - core), f),
        "x": (d, 1 - f),
        "y": (at(z, 1 - y, core), f),
    }
    for k in range(1, NZ):
        peers["z%d" % k] = (at(lax.rem(z + k, NZ), y, core), f)
    return f, core, y, z, peers


def norm_parts(v):
    c = v - jnp.mean(v, axis=-1, keepdims=True)
    r = lax.rsqrt(jnp.mean(c * c, axis=-1, keepdims=True) + EPS)
    return c * r, r


def layer_kernel(
    counts, tok, cot, w0, w1, w2, w3, s_in,
    res, gtok, gdown, gup, gqo, gsmall,
    tokv, cotv, xs, dys, h, lt, qkv, o, lse, x1, gact, dact, dh, vec, smv,
    v0, v1, v2, v3,
    own, snd, ownd, sndd,
    cb, xb, yb, zb, stg, cbd, xbd, ybd, zbd, stgd, sacc, srecv,
    gxs, gys, gcs, gzs, gzcs, lsem, csem, xsem, ysem, zsem, azsem, aysem, acsem, psem, ssem,
):
    f, core, y, z, peers = places()
    ins = (w0, w1, w2, w3)
    ws = (v0, v1, v2, v3)
    barrier = pltpu.get_barrier_semaphore()
    for name in peers:
        pl.semaphore_signal(barrier, inc=1, device_id=peers[name], device_id_type=MESH)

    def send(src, dst, sems, idx, name):
        return pltpu.make_async_remote_copy(
            src_ref=src, dst_ref=dst, send_sem=sems.at[(0,) + idx], recv_sem=sems.at[(1,) + idx],
            device_id=peers[name], device_id_type=MESH,
        )

    def piece(g, half, yy, zz=None):
        w, r0, rows = PIECES[g]
        full = ins[w].shape[0]
        quarter = core * 2 + yy
        if g == SHARED:
            start = half * full + (z if zz is None else zz) * (full // 4) + quarter * rows
        else:
            start = half * full + quarter * (full // 4) + r0
        return w, pl.ds(pl.multiple_of(start, 16), rows)

    def gx(g):
        w, there = piece(g, f, y)
        _, here = piece(g, 0, y)
        return send(ins[w].at[here], ws[w].at[there], gxs, (g,), "x")

    def gy(g):
        w, at = piece(g, 1 - f, y)
        return send(ws[w].at[at], ws[w].at[at], gys, (g,), "y")

    def gc(g, k):
        w, at = piece(g, 1 - f, y if k == 0 else 1 - y)
        return send(ws[w].at[at], ws[w].at[at], gcs, (g, k), "c")

    def gz(e, k):
        w, at = piece(SHARED, 1 - f, y if e == 0 else 1 - y)
        return send(ws[w].at[at], ws[w].at[at], gzs, (e, k - 1), "z%d" % k)

    def gzc(k):
        start = (1 - f) * (FF // 2) + lax.rem(z + NZ - k, NZ) * (FF // 8) + core * (FF // 16)
        at = pl.ds(pl.multiple_of(start, 16), FF // 16)
        return send(v3.at[at], v3.at[at], gzcs, (k - 1,), "c")

    def got_x(g):
        gx(g).wait()
        if g + GW < len(PIECES):
            gx(g + GW).start()
        gy(g).start()
        gc(g, 0).start()
        if g == SHARED:
            for k in range(1, NZ):
                gz(0, k).start()

    def got_y(g):
        gy(g).wait()
        gc(g, 1).start()
        if g == SHARED:
            for k in range(1, NZ):
                gz(1, k).start()

    def got_xy(g):
        if g < len(PIECES):
            got_x(g)
        if g >= GLAG:
            got_y(g - GLAG)

    def got_z(k):
        gz(0, k).wait()
        gz(1, k).wait()
        gzc(k).start()

    def got(w):
        for g in range(len(PIECES)):
            if PIECES[g][0] == w:
                gc(g, 0).wait()
                gc(g, 1).wait()
        if w == 3:
            for k in range(1, NZ):
                gzc(k).wait()
        local[w].wait()

    rows_in = (pltpu.make_async_copy(tok, tokv, lsem.at[5]), pltpu.make_async_copy(cot, cotv, lsem.at[6]))
    rows_in[0].start()
    local = []
    for i in range(4):
        full = ins[i].shape[0]
        local.append(pltpu.make_async_copy(ins[i], ws[i].at[pl.ds(pl.multiple_of(f * full, 16), full)], lsem.at[i]))
    local.append(pltpu.make_async_copy(s_in, smv.at[f], lsem.at[4]))
    local[4].start()
    pl.semaphore_wait(barrier, len(peers))
    small_x = send(s_in, smv.at[f], ssem, (6,), "x")
    small_x.start()
    for g in range(GW):
        gx(g).start()
    rows_in[1].start()
    for i in range(4):
        local[i].start()

    def c_copy(i, down):
        if down:
            return send(sndd.at[lax.rem(i, 3)], cbd.at[i], csem, (i,), "c")
        return send(snd.at[lax.rem(i, 3)], cb.at[i - 6], csem, (i,), "c")

    def bufs(i):
        if i < 6:
            return i, 128, D, cbd, xbd, ybd, zbd, stgd
        return i - 6, HALF, 256, cb, xb, yb, zb, stg

    def x_copy(n):
        i, e = n // 2, n % 2
        j, ur, uc, cc, xx, _, _, _ = bufs(i)
        half = ds(((1 - y) if e == 0 else y) * (ur // 2), ur // 2)
        return send(cc.at[j, 1 - f, half], xx.at[j, half], xsem, (i, e), "x")

    def y_copy(i):
        j, ur, uc, _, xx, yy, _, _ = bufs(i)
        return send(xx.at[j, ds((1 - y) * (ur // 2), ur // 2)], yy.at[j], ysem, (i,), "y")

    def z_copy(i, k):
        j, ur, uc, _, _, yy, zz, _ = bufs(i)
        return send(
            yy.at[j, ds(lax.rem(z + k, NZ) * (ur // 8), ur // 8)], zz.at[j, k - 1], zsem, (i, k - 1), "z%d" % k
        )

    def outpart(i, start, rows):
        j = i % 6 if i < 12 else (i - 12 + 5) % 6
        if i < 6:
            return gdown.at[pl.ds(pl.multiple_of((2 * j + core) * 128 + start, 16), rows), :]
        ref = gup if i < 12 else gqo
        return ref.at[pl.ds(mult(start, 16), rows), ds((2 * j + core) * 256, 256)]

    def own_piece(i):
        j, ur, uc, _, _, _, _, st = bufs(i)
        return outpart(i, y * (ur // 2) + z * (ur // 8), ur // 8), st.at[j]

    def p_copy(i):
        dst, src = own_piece(i)
        return pltpu.make_async_copy(src, dst, psem.at[i])

    def az_copy(i, k):
        dst, src = own_piece(i)
        return send(src, dst, azsem, (i, k - 1), "z%d" % k)

    def ay_copy(i):
        ur = 128 if i < 6 else HALF
        part = outpart(i, y * (ur // 2), ur // 2)
        return send(part, part, aysem, (i,), "y")

    def ac_copy(i):
        ur = 128 if i < 6 else HALF
        part = outpart(i, 0, ur)
        return send(part, part, acsem, (i,), "c")

    def s1(i, down):
        c_copy(i, down).wait()
        if down:
            cbd[i] = (cbd[i].astype(F32) + ownd[lax.rem(i, 3)].astype(F32)).astype(BF16)
        else:
            cb[i - 6] = (cb[i - 6].astype(F32) + own[lax.rem(i, 3)].astype(F32)).astype(BF16)

    def s2(n):
        x_copy(n).wait()
        i = n // 2
        if n % 2 == 0:
            j, ur, uc, cc, xx, _, _, _ = bufs(i)
            half = ds((1 - y) * (ur // 2), ur // 2)
            xx[j, half] = (xx[j, half].astype(F32) + cc[j, f, half].astype(F32)).astype(BF16)
            y_copy(i).start()

    def s3(i):
        y_copy(i).wait()
        j, ur, uc, cc, xx, yy, _, _ = bufs(i)
        half = ds(y * (ur // 2), ur // 2)
        yy[j] = (yy[j].astype(F32) + (xx[j, half].astype(F32) + cc[j, f, half].astype(F32))).astype(BF16)
        for k in range(1, NZ):
            z_copy(i, k).start()

    def s4(i):
        for k in range(1, NZ):
            z_copy(i, k).wait()
        j, ur, uc, _, _, yy, zz, st = bufs(i)
        total = yy[j, ds(z * (ur // 8), ur // 8)].astype(F32)
        for k in range(1, NZ):
            total = total + zz[j, k - 1].astype(F32)
        st[j] = total.astype(BF16)
        p_copy(i).start()
        for k in range(1, NZ):
            az_copy(i, k).start()

    def s5(i):
        p_copy(i).wait()
        for k in range(1, NZ):
            az_copy(i, k).wait()
        ay_copy(i).start()

    def s6(i):
        ay_copy(i).wait()
        ac_copy(i).start()

    def s7(i):
        ac_copy(i).wait()

    def slot(n):
        if n < 2 * NCH:
            s2(n)
        for lag, stage in ((3, s3), (6, s4), (9, s5), (12, s6), (15, s7)):
            if (n - lag) % 2 == 0 and 0 <= (n - lag) // 2 < NCH:
                stage((n - lag) // 2)

    def point(name):
        for what, n in PLAN[name]:
            if what == "start":
                x_copy(n).start()
            else:
                slot(n)

    rows_in[0].wait()
    for p in range(PAIRS):
        xs[p * LPAD : p * LPAD + LENGTH] = tokv[p].astype(F32)
        xs[p * LPAD + LENGTH : (p + 1) * LPAD] = jnp.zeros((LPAD - LENGTH, D), F32)

    local[4].wait()
    small_x.wait()
    s0 = smv[0].astype(F32)
    s1v = smv[1].astype(F32)
    for j, r in enumerate((G1, B1, OB, G2, B2, DB)):
        vec[j] = jnp.concatenate([s0[r : r + 1], s1v[r : r + 1]], axis=1)
    vec[6] = jnp.concatenate([s0[QV : QV + 1], s0[QV + 1 : QV + 2]], axis=1)
    vec[7] = jnp.zeros((1, D), F32)
    vec[8] = jnp.concatenate([s1v[QV : QV + 1], s1v[QV + 1 : QV + 2]], axis=1)
    vec[9] = jnp.concatenate([s0[UB : UB + 1], s0[UB + 1 : UB + 2]], axis=1)
    vec[10] = jnp.concatenate([s0[UB + 2 : UB + 3], s0[UB + 3 : UB + 4]], axis=1)
    vec[11] = jnp.concatenate([s1v[UB : UB + 1], s1v[UB + 1 : UB + 2]], axis=1)
    vec[12] = jnp.concatenate([s1v[UB + 2 : UB + 3], s1v[UB + 3 : UB + 4]], axis=1)

    def loop(n, body):
        def step(i, carry):
            body(i)
            return carry

        lax.fori_loop(0, n, step, 0)

    def transpose_into(src, k):
        def body(j):
            cols = ds(j * 128, 128)
            lt[k, cols, :] = src[:, cols].astype(F32).T.astype(BF16)

        loop(D // 128, body)

    def ln1(i):
        rows = ds(i * 96, 96)
        n, _ = norm_parts(xs[rows])
        h[rows] = (n * vec[0] + vec[1]).astype(BF16)

    loop(6, ln1)
    got_xy(0)
    got_xy(1)
    transpose_into(h, 0)
    got_xy(2)
    rows_in[1].wait()
    for p in range(PAIRS):
        dys[p * LPAD : (p + 1) * LPAD] = jnp.concatenate(
            [cotv[p].astype(F32), jnp.zeros((LPAD - LENGTH, D), F32)], axis=0
        ).astype(BF16)
    for g in range(3, 6 + GLAG):
        got_xy(g)
    got(0)

    def qkv_body(i):
        cols = ds(i * D, D)
        qkv[:, cols] = (dot(h[...], v0[:, cols]) + vec[6 + i]).astype(BF16)

    loop(3, qkv_body)
    lane = lax.broadcasted_iota(jnp.int32, (1, 128), 1)
    low = lane < 64
    key = lax.broadcasted_iota(jnp.int32, (1, LPAD), 1)

    def attend(i):
        for when, gs in enumerate(GATHER_AT):
            if gs:
                pl.when(i == when)(lambda gs=gs: [got_xy(g) for g in gs] and None)
        p = i // 6
        hp = lax.rem(i, 6)
        rows = ds(p * LPAD, LPAD)
        q = qkv[rows, ds(hp * 128, 128)].astype(F32) * 0.125
        k = qkv[rows, ds(D + hp * 128, 128)]
        v = qkv[rows, ds(2 * D + hp * 128, 128)]
        valid = key < TEXT + counts[p]
        outs = []
        ls = lse[rows]
        for e in range(2):
            qm = jnp.where(low if e == 0 else jnp.logical_not(low), q, 0.0).astype(BF16)
            s = jnp.where(valid, dot_nt(qm, k), -1e30)
            m = jnp.max(s, axis=-1, keepdims=True)
            ex = jnp.exp(s - m)
            t = jnp.sum(ex, axis=-1, keepdims=True)
            ls = jnp.where(lane == 2 * hp + e, m + jnp.log(t), ls)
            outs.append(dot((ex / t).astype(BF16), v))
        lse[rows] = ls
        o[rows, ds(hp * 128, 128)] = jnp.where(low, outs[0], outs[1]).astype(BF16)

    loop(12, attend)
    got(1)

    def proj(i):
        cols = ds(i * 256, 256)
        x1[:, cols] = xs[:, cols] + dot(o[...], v1[:, cols]) + vec[2, :, cols]

    loop(3, proj)

    def ln2(i):
        rows = ds(i * 96, 96)
        n, _ = norm_parts(x1[rows])
        h[rows] = (n * vec[3] + vec[4]).astype(BF16)

    loop(6, ln2)
    transpose_into(o, 1)
    transpose_into(h, 2)
    got(2)

    def up_tile(j):
        cols = ds(j * 256, 256)
        u = dot(h[...], v2[:, cols]) + vec[9 + j // 3, :, ds(lax.rem(j, 3) * 256, 256)]
        phi = 0.5 * (1.0 + lax.erf(u * 0.7071067811865476))
        gact[:, cols] = (u * phi).astype(BF16)
        dact[:, cols] = (phi + u * (0.3989422804014327 * jnp.exp(-0.5 * u * u))).astype(BF16)

    def down_chunk(i):
        par = lax.rem(i, 3)
        for x in range(2):
            cols = x * (FF // 2) + i * 256
            mine = gact[:, ds(cols + core * 128, 128)]
            other = gact[:, ds(cols + (1 - core) * 128, 128)]
            both = jnp.concatenate([mine, other], axis=1)
            for n in range(3):
                r = dot_tn(both, dys[:, n * 256 : (n + 1) * 256]).astype(BF16)
                ownd[par, x, :, n * 256 : (n + 1) * 256] = r[:128]
                sndd[par, x, :, n * 256 : (n + 1) * 256] = r[128:]
        c_copy(i, True).start()

    def phase_a(i):
        up_tile(i)
        up_tile(6 + i)

        @pl.when(i > 1)
        def _():
            s1(i - 2, True)

        for when in range(2, 6):
            pl.when(i == when)(functools.partial(point, "A%d" % when))
        for k in range(1, NZ):
            pl.when(i == k + 2)(functools.partial(got_z, k))
        down_chunk(i)

    loop(6, phase_a)
    got(3)

    def down_proj(n):
        cols = ds(n * 256, 256)
        r = (x1[:, cols] + dot(gact[...], v3[:, cols]) + vec[5, :, cols])
        for p in range(PAIRS):
            tokv[p, :, cols] = r[p * LPAD : p * LPAD + LENGTH].astype(BF16)

    loop(3, down_proj)
    result_out = pltpu.make_async_copy(tokv, res, lsem.at[5])
    result_out.start()
    s1(4, True)
    s1(5, True)
    point("B")

    def du_tile(j):
        cols = ds(j * 256, 256)
        du = (dot_nt(dys[...], v3[cols, :]) * dact[:, cols].astype(F32)).astype(BF16)
        dact[:, cols] = du
        sums = jnp.sum(du.astype(F32), axis=0, keepdims=True)
        for e in range(2):
            sacc[j // 6, 3 * UB + 2 * lax.rem(j, 6) + e] = sums[:, e * 128 : (e + 1) * 128]

    def col_chunk(i, j, sel, src):
        par = lax.rem(i, 3)
        for side, dst in ((core, own), (1 - core, snd)):
            u = 2 * j + side
            col_unit(dst, par, u, sel, src)
        c_copy(i, False).start()

    def col_unit(dst, par, u, sel, src):
        r = dot(lt[sel], src[:, ds(u * 256, 256)]).astype(BF16)
        dst[par, 0] = r[:HALF]
        dst[par, 1] = r[HALF:]

    def phase_c(j):
        du_tile(2 * j)
        du_tile(2 * j + 1)

        @pl.when(j > 1)
        def _():
            s1(4 + j, False)

        for when in range(6):
            pl.when(j == when)(functools.partial(point, "C%d" % when))
        col_chunk(6 + j, j, 2, dact)

    loop(6, phase_c)

    def dh2_tile(n):
        cols = ds(n * 256, 256)
        dh[:, cols] = dot_nt(dact[...], v2[cols, :])

    loop(3, dh2_tile)
    s1(10, False)
    s1(11, False)
    point("D")
    zero = jnp.zeros((1, D), F32)

    def spread(x, r, v):
        for j in range(v.shape[1] // 128):
            sacc[x, 3 * r + j] = v[:, j * 128 : (j + 1) * 128]

    def put(r, v):
        spread(0, r, v[:, :HALF])
        spread(1, r, v[:, HALF:])

    def ln2_back(i, carry):
        a, b, c2, d2 = carry
        rows = ds(i * 96, 96)
        n, r = norm_parts(x1[rows])
        g = dh[rows]
        e = g * vec[3]
        dy = dys[rows].astype(F32)
        dx = dy + r * (
            e - jnp.mean(e, axis=-1, keepdims=True) - n * jnp.mean(e * n, axis=-1, keepdims=True)
        )
        x1[rows] = dx
        da = dx.astype(BF16)
        qkv[rows, 3 * D :] = da
        return (
            a + jnp.sum(g * n, axis=0, keepdims=True),
            b + jnp.sum(g, axis=0, keepdims=True),
            c2 + jnp.sum(da.astype(F32), axis=0, keepdims=True),
            d2 + jnp.sum(dy, axis=0, keepdims=True),
        )

    sums = lax.fori_loop(0, 6, ln2_back, (zero, zero, zero, zero))
    for r, v in zip((G2, B2, OB, DB), sums):
        put(r, v)

    col_chunk(12, 5 + core // 2, 1, qkv)

    point("E0")

    def do_tile(n):
        cols = ds(n * 256, 256)
        o[:, cols] = dot_nt(qkv[:, 3 * D :], v1[cols, :]).astype(BF16)

    loop(3, do_tile)
    s1(12, False)
    point("E")

    def attend_back(i):
        for when in range(12):
            pl.when(i == when)(functools.partial(point, "F%d" % when))
        p = i // 6
        hp = lax.rem(i, 6)
        rows = ds(p * LPAD, LPAD)
        q = qkv[rows, ds(hp * 128, 128)]
        k = qkv[rows, ds(D + hp * 128, 128)]
        v = qkv[rows, ds(2 * D + hp * 128, 128)]
        g = o[rows, ds(hp * 128, 128)]
        qf = q.astype(F32) * 0.125
        gf = g.astype(F32)
        valid = key < TEXT + counts[p]
        ls = lse[rows]
        got3 = []
        for e in range(2):
            keep = low if e == 0 else jnp.logical_not(low)
            qm = jnp.where(keep, qf, 0.0).astype(BF16)
            gm = jnp.where(keep, gf, 0.0).astype(BF16)
            total = jnp.sum(jnp.where(lane == 2 * hp + e, ls, 0.0), axis=-1, keepdims=True)
            pr = jnp.where(valid, jnp.exp(dot_nt(qm, k) - total), 0.0)
            dp = dot_nt(gm, v)
            dsc = (pr * (dp - jnp.sum(pr * dp, axis=-1, keepdims=True))).astype(BF16)
            got3.append((dot(dsc, k), dot_tn(dsc, q), dot_tn(pr.astype(BF16), g)))
        for part, scale in ((0, 0.125), (1, 0.125), (2, 1.0)):
            r = jnp.where(low, got3[0][part], got3[1][part]) * scale
            qkv[rows, ds(part * D + hp * 128, 128)] = r.astype(BF16)

    loop(12, attend_back)

    def phase_g(t):
        @pl.when(t > 1)
        def _():
            s1(11 + t, False)

        for when in range(2, 4):
            pl.when(t == when)(functools.partial(point, "G%d" % when))
        col_chunk(13 + t, t, 0, qkv)

    loop(4, phase_g)
    for c in range(2):

        @pl.when(core == c)
        def _():
            for side, dst in ((c, own), (1 - c, snd)):
                col_unit(dst, 17 % 3, 8 + side, side, qkv)

    c_copy(17, False).start()
    s1(15, False)
    point("G4")

    def dh1_tile(n):
        cols = ds(n * 256, 256)
        dh[:, cols] = dot_nt(qkv[:, : 3 * D], v0[cols, :])

    loop(3, dh1_tile)
    s1(16, False)
    s1(17, False)
    point("H")

    def ln1_back(i, carry):
        a, b, qs, vs = carry
        rows = ds(i * 96, 96)
        n, r = norm_parts(xs[rows])
        g = dh[rows]
        e = g * vec[0]
        xs[rows] = x1[rows] + r * (
            e - jnp.mean(e, axis=-1, keepdims=True) - n * jnp.mean(e * n, axis=-1, keepdims=True)
        )
        return (
            a + jnp.sum(g * n, axis=0, keepdims=True),
            b + jnp.sum(g, axis=0, keepdims=True),
            qs + jnp.sum(qkv[rows, :D].astype(F32), axis=0, keepdims=True),
            vs + jnp.sum(qkv[rows, 2 * D : 3 * D].astype(F32), axis=0, keepdims=True),
        )

    ga, gb, qs, vs = lax.fori_loop(0, 6, ln1_back, (zero, zero, zero, zero))
    put(G1, ga)
    put(B1, gb)
    for x, v in ((0, qs), (1, vs)):
        spread(x, QV, v)
    for p in range(PAIRS):
        cotv[p] = xs[p * LPAD : p * LPAD + LENGTH].astype(BF16)
    grad_out = pltpu.make_async_copy(cotv, gtok, lsem.at[6])
    grad_out.start()
    point("I")

    n = POINTS[-1][2]
    for j, name in enumerate(("c", "x", "y")):
        cp = send(sacc, srecv.at[j], ssem, (j,), name)
        cp.start()
        for _ in range(2):
            point("Z%d" % n)
            n += 1
        cp.wait()
        sacc[...] = sacc[...] + srecv[j]
    copies = [send(sacc, srecv.at[3 + z], ssem, (2 + k,), "z%d" % k) for k in range(1, NZ)]
    for cp in copies:
        cp.start()
    srecv[3 + z] = sacc[...]
    for _ in range(2):
        point("Z%d" % n)
        n += 1
    for cp in copies:
        cp.wait()
    gsmall[...] = (srecv[3, f] + srecv[4, f]) + (srecv[5, f] + srecv[6, f])
    while n < SLOTS:
        point("Z%d" % n)
        n += 1
    result_out.wait()
    grad_out.wait()


def layer(*arrays):
    vm = pltpu.VMEM
    dma = pltpu.SemaphoreType.DMA
    any_ = pl.BlockSpec(memory_space=pl.ANY)
    inside = pl.BlockSpec(memory_space=pltpu.VMEM)
    pieces = len(PIECES)
    return pl.pallas_call(
        layer_kernel,
        out_shape=[
            jax.ShapeDtypeStruct((PAIRS, LENGTH, D), BF16),
            jax.ShapeDtypeStruct((PAIRS, LENGTH, D), BF16),
            jax.ShapeDtypeStruct((FF // 2, D), BF16),
            jax.ShapeDtypeStruct((HALF, FF), BF16),
            jax.ShapeDtypeStruct((HALF, FF), BF16),
            jax.ShapeDtypeStruct((36, 1, 128), F32),
        ],
        in_specs=[pl.BlockSpec(memory_space=pltpu.SMEM)] + [any_] * 7,
        out_specs=[any_] * 5 + [inside],
        scratch_shapes=[
            vm((PAIRS, LENGTH, D), BF16),
            vm((PAIRS, LENGTH, D), BF16),
            vm((ROWS, D), F32),
            vm((ROWS, D), BF16),
            vm((ROWS, D), BF16),
            vm((3, D, ROWS), BF16),
            vm((ROWS, 4 * D), BF16),
            vm((ROWS, D), BF16),
            vm((ROWS, 128), F32),
            vm((ROWS, D), F32),
            vm((ROWS, FF), BF16),
            vm((ROWS, FF), BF16),
            vm((ROWS, D), F32),
            vm((13, 1, D), F32),
            vm((2, 16, HALF), BF16),
            vm((D, 3 * D), BF16),
            vm((D, D), BF16),
            vm((D, FF), BF16),
            vm((FF, D), BF16),
            vm((3, 2, HALF, 256), BF16),
            vm((3, 2, HALF, 256), BF16),
            vm((3, 2, 128, D), BF16),
            vm((3, 2, 128, D), BF16),
            vm((12, 2, HALF, 256), BF16),
            vm((12, HALF, 256), BF16),
            vm((12, HALF // 2, 256), BF16),
            vm((12, NZ - 1, HALF // 8, 256), BF16),
            vm((12, HALF // 8, 256), BF16),
            vm((6, 2, 128, D), BF16),
            vm((6, 128, D), BF16),
            vm((6, 64, D), BF16),
            vm((6, NZ - 1, 16, D), BF16),
            vm((6, 16, D), BF16),
            vm((2, 36, 1, 128), F32),
            vm((7, 2, 36, 1, 128), F32),
            dma((2, pieces)),
            dma((2, pieces)),
            dma((2, pieces, 2)),
            dma((2, 2, NZ - 1)),
            dma((2, NZ - 1)),
            dma((7,)),
            dma((2, NCH)),
            dma((2, NCH, 2)),
            dma((2, NCH)),
            dma((2, NCH, NZ - 1)),
            dma((2, NCH, NZ - 1)),
            dma((2, NCH)),
            dma((2, NCH)),
            dma((NCH,)),
            dma((2, 7)),
        ],
        compiler_params=pltpu.CompilerParams(
            collective_id=1, has_side_effects=True, vmem_limit_bytes=63 << 20
        ),
        name="layer",
    )(*arrays)


def finish_kernel(gdown, gup, gqo, gsmall, res, gtok, down, up, qkv, out, res_out, gtok_out, *vectors):
    down[...] = gdown[...].astype(F32)
    up[...] = gup[...].astype(F32)
    qkv[...] = gqo[:, : 3 * D].astype(F32)
    out[...] = gqo[:, 3 * D :].astype(F32)
    res_out[...] = res[...]
    gtok_out[...] = gtok[...]

    @pl.when(pl.program_id(0) == 0)
    def _():
        at = 0
        for v in vectors:
            n = v.shape[0] // 128
            for j in range(n):
                v[j * 128 : (j + 1) * 128] = gsmall[at + j, 0]
            at += n


def finish(gdown, gup, gqo, gsmall, res, gtok):
    steps = 8
    rows = PAIRS * LENGTH // 7

    def cut(n, width):
        return pl.BlockSpec((n, width), lambda i: (i, 0))

    tokens = pl.BlockSpec((rows, D), lambda i: (jnp.minimum(i, 6), 0))
    out = pl.pallas_call(
        finish_kernel,
        grid=(steps,),
        out_shape=[
            jax.ShapeDtypeStruct((FF // 2, D), F32),
            jax.ShapeDtypeStruct((HALF, FF), F32),
            jax.ShapeDtypeStruct((HALF, 3 * D), F32),
            jax.ShapeDtypeStruct((HALF, D), F32),
            jax.ShapeDtypeStruct((PAIRS * LENGTH, D), BF16),
            jax.ShapeDtypeStruct((PAIRS * LENGTH, D), BF16),
        ]
        + [jax.ShapeDtypeStruct((n * HALF,), F32) for n in SMALL],
        in_specs=[
            cut(FF // 2 // steps, D),
            cut(HALF // steps, FF),
            cut(HALF // steps, FF),
            pl.BlockSpec((36, 1, 128), lambda i: (0, 0, 0)),
            tokens,
            tokens,
        ],
        out_specs=[
            cut(FF // 2 // steps, D),
            cut(HALF // steps, FF),
            cut(HALF // steps, 3 * D),
            cut(HALF // steps, D),
            tokens,
            tokens,
        ]
        + [pl.BlockSpec((n * HALF,), lambda i: (0,)) for n in SMALL],
        name="finish",
    )(gdown, gup, gqo, gsmall, res.reshape(PAIRS * LENGTH, D), gtok.reshape(PAIRS * LENGTH, D))
    return out


def on_device(extra, tokens, patch_counts, cotangent, norm1_gain, norm1_bias, qkv_weight, qv_bias,
              out_weight, out_bias, norm2_gain, norm2_bias, up_weight, up_bias, down_weight, down_bias):
    small, at = 0, 0
    for v in (norm1_gain, norm1_bias, qv_bias, out_bias, norm2_gain, norm2_bias, up_bias, down_bias):
        small = small + jnp.pad(v, (at, 16 * HALF - at - v.size))
        at += v.size
    small = small.reshape(16, HALF)
    result, grad_tokens, gdown, gup, gqo, gsmall = layer(
        patch_counts, tokens, cotangent, qkv_weight, out_weight, up_weight, down_weight, small
    )
    down, up, qkv, out, result, grad_tokens, *parts = finish(gdown, gup, gqo, gsmall, result, grad_tokens)
    grads = [down, up, qkv, out] + parts
    if extra is not None:
        grads = lax.psum(grads, "dp", axis_index_groups=extra)
    down, up, qkv, out, *parts = grads
    result, grad_tokens = (v.reshape(PAIRS, LENGTH, D) for v in (result, grad_tokens))
    return (
        result, grad_tokens, parts[0], parts[1], qkv, parts[2], out, parts[3],
        parts[4], parts[5], up, parts[6], down, parts[7],
    )


def solution(mesh):
    dp = mesh.shape["dp"]
    extra = None
    if dp > GROUP:
        extra = [[j + GROUP * i for i in range(dp // GROUP)] for j in range(GROUP)]
    row = P(("dp", "fsdp"), None, None)
    vec = P("fsdp")
    mat = P("fsdp", None)
    return jax.shard_map(
        functools.partial(on_device, extra),
        mesh=mesh,
        in_specs=(row, P(("dp", "fsdp")), row, vec, vec, mat, vec, mat, vec, vec, vec, mat, vec, mat, vec),
        out_specs=(row, row, vec, vec, mat, vec, mat, vec, vec, vec, mat, vec, mat, vec),
        check_vma=False,
    )
```

```python
import functools

import jax
import jax.numpy as jnp
from jax import lax
from jax.experimental import pallas as pl
from jax.experimental.pallas import tpu as pltpu
from jax.sharding import PartitionSpec as P

TEXT = 40
MESH = pl.DeviceIdType.MESH
BF16 = jnp.bfloat16
F32 = jnp.float32
EPS = 1e-06
NZ = 4
GROUP = 16
PAIRS = 2
LENGTH = 280
LPAD = 288
ROWS = PAIRS * LPAD
D = 768
FF = 3072
HALF = D // 2
NCH = 18
GW = 5
PIECES = (
    [(2, 4, 0, 96, FF // 2, FF // 8, 0, FF // 8)]
    + [(0, j, 0, 96, k * D + j * 256, 256, 0, 0) for j in range(3) for k in range(3)]
    + [(1, 3, 48 * j, 48, 0, D, 0, 0) for j in range(2)]
    + [(2, 4, 0, 96, 384 * j, 384, 0, 0) for j in range(4)]
    + [(3, 5, 0, 48, 0, D, 48, 0)]
    + [(3, 5, 192 + 96 * j, 96, 0, D, 0, 0) for j in range(2)]
)
SHARED = [g for g, p in enumerate(PIECES) if p[6] or p[7]]
GLAG = 3
STEPS = len(PIECES) + GLAG
SMALL = (1, 1, 2, 1, 1, 1, 4, 1)
G1, B1, QV, OB, G2, B2, UB, DB = 0, 1, 2, 4, 5, 6, 7, 11


def plan():
    points = list(POINTS)
    points += [("Z%d" % n, NCH, n + 1) for n in range(points[-1][2], SLOTS)]
    acts, done, started = {}, 0, 0
    for name, ready, upto in points:
        todo = acts[name] = []
        while True:
            ahead = AHEAD if done < NARROW else AHEAD_LAST
            while started < min(2 * NCH, 2 * ready, done + ahead):
                todo.append(("start", started))
                started += 1
            if done == upto:
                break
            assert done >= 2 * NCH or started > done
            todo.append(("slot", done))
            done += 1
    return acts


POINTS = (
    ("A2", 1, 0), ("A3", 2, 1), ("A4", 3, 2), ("A5", 4, 3), ("B", 6, 5), ("C0", 6, 6), ("C1", 6, 6), ("C2", 7,
    7), ("C3", 8, 8), ("C4", 9, 9), ("C5", 10, 10), ("D", 12, 11), ("E0", 12, 12), ("E", 13, 13), ("F0", 13,
    13), ("F1", 13, 14), ("F2", 13, 14), ("F3", 13, 15), ("F4", 13, 16), ("F5", 13, 16), ("F6", 13, 17),
    ("F7", 13, 17), ("F8", 13, 18), ("F9", 13, 18), ("F10", 13, 19), ("F11", 13, 20), ("G2", 14, 21), ("G3",
    15, 22), ("G4", 16, 23), ("H", 18, 24), ("I", 18, 25),
)
SLOTS = 2 * NCH + 11
AHEAD, AHEAD_LAST, NARROW = 6, 6, 24
PLAN = plan()


def dot(a, b):
    return jnp.dot(a, b, preferred_element_type=F32)


def dot_nt(a, b):
    return lax.dot_general(a, b, (((1,), (1,)), ((), ())), preferred_element_type=F32)


def dot_tn(a, b):
    return lax.dot_general(a, b, (((0,), (0,)), ((), ())), preferred_element_type=F32)


def mult(x, n):
    return x if isinstance(x, int) else pl.multiple_of(x, n)


def ds(start, size, n=None):
    return pl.ds(mult(start, n or size), size)


def places():
    d = lax.axis_index("dp")
    f = lax.axis_index("fsdp")
    core = lax.rem(d, 2)
    y = lax.rem(d // 2, 2)
    z = lax.rem(d // 4, NZ)
    base = d - lax.rem(d, GROUP)

    def at(zz, yy, cc):
        return base + zz * 4 + yy * 2 + cc

    peers = {
        "c": (at(z, y, 1 - core), f),
        "x": (d, 1 - f),
        "y": (at(z, 1 - y, core), f),
    }
    for k in range(1, NZ):
        peers["z%d" % k] = (at(lax.rem(z + k, NZ), y, core), f)
    return f, core, y, z, peers


def norm_parts(v):
    c = v - jnp.mean(v, axis=-1, keepdims=True)
    r = lax.rsqrt(jnp.mean(c * c, axis=-1, keepdims=True) + EPS)
    return c * r, r


def layer_kernel(
    counts, tok, cot, w0, w1, w2, w3, s_in,
    res, gtok, gdown, gup, gqo, gsmall,
    tokv, cotv, xs, dys, h, lt, qkv, o, lse, x1, gact, dact, dh, vec, smv,
    v0, v1, v2, v3,
    own, snd, ownd, sndd,
    cb, xb, yb, zb, stg, cbd, xbd, ybd, zbd, stgd, sacc, srecv,
    gxs, gys, gcs, gzs, gsent, lsem, csent, rsent, csem, xsem, ysem, zsem, azsem, aysem, acsem, psem, ssem,
):
    f, core, y, z, peers = places()
    ins = (w0, w1, w2, w3)
    ws = (v0, v1, v2, v3)
    barrier = pltpu.get_barrier_semaphore()
    for name in peers:
        pl.semaphore_signal(barrier, inc=1, device_id=peers[name], device_id_type=MESH)

    def send(src, dst, sent, arrived, name):
        return pltpu.make_async_remote_copy(
            src_ref=src, dst_ref=dst, send_sem=sent, recv_sem=arrived,
            device_id=peers[name], device_id_type=MESH,
        )

    def piece(g, half, yy, zz=None):
        w, _, r0, rows, c0, cols, zr, zc = PIECES[g]
        full = ins[w].shape[0]
        zz = z if zz is None else zz
        start = half * full + (core * 2 + yy) * (full // 4) + r0 + zz * zr
        return w, (pl.ds(pl.multiple_of(start, 16), rows), ds(c0 + zz * zc, cols, 128))

    def same(g, yy, zz, sent, arrived, name):
        w, at = piece(g, 1 - f, yy, zz)
        return send(ws[w].at[at], ws[w].at[at], sent, arrived, name)

    def gx(g):
        w, there = piece(g, f, y)
        _, here = piece(g, 0, y)
        return send(ins[w].at[here], ws[w].at[there], gsent.at[0], gxs.at[g], "x")

    def gy(g):
        return same(g, y, z, gsent.at[1], gys.at[g], "y")

    def gc(g, e, k=0):
        arrived = gcs.at[PIECES[g][1]]
        return same(g, y if e == 0 else 1 - y, lax.rem(z + NZ - k, NZ), gsent.at[2], arrived, "c")

    def gz(g, e, k):
        return same(g, y if e == 0 else 1 - y, z, gsent.at[3], gzs.at[SHARED.index(g), k - 1, e], "z%d" % k)

    def got_x(g):
        gx(g).wait_recv()
        if g + GW < len(PIECES):
            gx(g + GW).start()
        gy(g).start()
        gc(g, 0).start()
        if g in SHARED:
            for k in range(1, NZ):
                gz(g, 0, k).start()

    def got_y(g):
        gy(g).wait_recv()
        gc(g, 1).start()
        if g in SHARED:
            for k in range(1, NZ):
                gz(g, 1, k).start()

    def step(n):
        if n < len(PIECES):
            got_x(n)
        if n >= GLAG:
            got_y(n - GLAG)

    def steps(first, last):
        for n in range(first, last + 1):
            step(n)

    def got_z(g, k):
        for e in range(2):
            gz(g, e, k).wait_recv()
            gc(g, e, k).start()

    def whole(sem, rows):
        at = v3.at[pl.ds(0, rows)]
        return send(at, at, sem, sem, "c")

    def got(j):
        whole(gcs.at[j], (192, 192, 192, 192, 768, 768)[j]).wait_recv()

    rows_in = (pltpu.make_async_copy(tok, tokv, lsem.at[5]), pltpu.make_async_copy(cot, cotv, lsem.at[6]))
    rows_in[0].start()
    local = []
    for i in range(4):
        full = ins[i].shape[0]
        local.append(pltpu.make_async_copy(ins[i], ws[i].at[pl.ds(pl.multiple_of(f * full, 16), full)], lsem.at[i]))
    local.append(pltpu.make_async_copy(s_in, smv.at[f], lsem.at[4]))
    local[4].start()
    pl.semaphore_wait(barrier, len(peers))
    small_x = send(s_in, smv.at[f], ssem.at[0, 6], ssem.at[1, 6], "x")
    small_x.start()
    for g in range(GW):
        gx(g).start()
    rows_in[1].start()
    for i in range(4):
        local[i].start()

    def c_copy(i, down):
        if down:
            return send(sndd.at[lax.rem(i, 3)], cbd.at[i], csent.at[lax.rem(i, 3)], csem.at[i], "c")
        return send(snd.at[lax.rem(i, 3)], cb.at[i - 6], csent.at[3 + lax.rem(i, 3)], csem.at[i], "c")

    def bufs(i):
        if i < 6:
            return i, 128, D, cbd, xbd, ybd, zbd, stgd
        return i - 6, HALF, 256, cb, xb, yb, zb, stg

    def x_copy(n):
        i, e = n // 2, n % 2
        j, ur, uc, cc, xx, _, _, _ = bufs(i)
        half = ds(((1 - y) if e == 0 else y) * (ur // 2), ur // 2)
        return send(cc.at[j, 1 - f, half], xx.at[j, half], rsent.at[0], xsem.at[n], "x")

    def y_copy(i):
        j, ur, uc, _, xx, yy, _, _ = bufs(i)
        return send(xx.at[j, ds((1 - y) * (ur // 2), ur // 2)], yy.at[j], rsent.at[1], ysem.at[i], "y")

    def z_copy(i, k):
        j, ur, uc, _, _, yy, zz, _ = bufs(i)
        return send(
            yy.at[j, ds(lax.rem(z + k, NZ) * (ur // 8), ur // 8)], zz.at[j, k - 1], rsent.at[2], zsem.at[i], "z%d" % k
        )

    def outpart(i, start, rows):
        j = i % 6 if i < 12 else (i - 12 + 5) % 6
        if i < 6:
            return gdown.at[pl.ds(pl.multiple_of((2 * j + core) * 128 + start, 16), rows), :]
        ref = gup if i < 12 else gqo
        return ref.at[pl.ds(mult(start, 16), rows), ds((2 * j + core) * 256, 256)]

    def own_piece(i):
        j, ur, uc, _, _, _, _, st = bufs(i)
        return outpart(i, y * (ur // 2) + z * (ur // 8), ur // 8), st.at[j]

    def p_copy(i):
        dst, src = own_piece(i)
        return pltpu.make_async_copy(src, dst, psem.at[i])

    def az_copy(i, k):
        dst, src = own_piece(i)
        return send(src, dst, rsent.at[3], azsem.at[i], "z%d" % k)

    def ay_copy(i):
        ur = 128 if i < 6 else HALF
        part = outpart(i, y * (ur // 2), ur // 2)
        return send(part, part, rsent.at[4], aysem.at[i], "y")

    def ac_copy(i):
        ur = 128 if i < 6 else HALF
        part = outpart(i, 0, ur)
        return send(part, part, rsent.at[5], acsem.at[0], "c")

    def s1(i, down):
        c_copy(i, down).wait()
        if down:
            cbd[i] = (cbd[i].astype(F32) + ownd[lax.rem(i, 3)].astype(F32)).astype(BF16)
        else:
            cb[i - 6] = (cb[i - 6].astype(F32) + own[lax.rem(i, 3)].astype(F32)).astype(BF16)

    def s2(n):
        x_copy(n).wait_recv()
        i = n // 2
        if n % 2 == 0:
            j, ur, uc, cc, xx, _, _, _ = bufs(i)
            half = ds((1 - y) * (ur // 2), ur // 2)
            xx[j, half] = (xx[j, half].astype(F32) + cc[j, f, half].astype(F32)).astype(BF16)
            y_copy(i).start()

    def s3(i):
        y_copy(i).wait_recv()
        j, ur, uc, cc, xx, yy, _, _ = bufs(i)
        half = ds(y * (ur // 2), ur // 2)
        yy[j] = (yy[j].astype(F32) + (xx[j, half].astype(F32) + cc[j, f, half].astype(F32))).astype(BF16)
        for k in range(1, NZ):
            z_copy(i, k).start()

    def s4(i):
        j, ur, uc, _, _, yy, zz, st = bufs(i)
        send(zz.at[j], zz.at[j], rsent.at[2], zsem.at[i], "z1").wait_recv()
        total = yy[j, ds(z * (ur // 8), ur // 8)].astype(F32)
        for k in range(1, NZ):
            total = total + zz[j, k - 1].astype(F32)
        st[j] = total.astype(BF16)
        p_copy(i).start()
        for k in range(1, NZ):
            az_copy(i, k).start()

    def s5(i):
        p_copy(i).wait()
        j, _, _, _, _, _, zz, _ = bufs(i)
        send(zz.at[j], zz.at[j], rsent.at[3], azsem.at[i], "z1").wait_recv()
        ay_copy(i).start()

    def s6(i):
        ay_copy(i).wait_recv()
        ac_copy(i).start()

    def slot(n):
        if n < 2 * NCH:
            s2(n)
        for lag, stage in ((3, s3), (6, s4), (9, s5), (12, s6)):
            if (n - lag) % 2 == 0 and 0 <= (n - lag) // 2 < NCH:
                stage((n - lag) // 2)

    def point(name):
        for what, n in PLAN[name]:
            if what == "start":
                x_copy(n).start()
            else:
                slot(n)

    rows_in[0].wait()
    for p in range(PAIRS):
        xs[p * LPAD : p * LPAD + LENGTH] = tokv[p].astype(F32)
        xs[p * LPAD + LENGTH : (p + 1) * LPAD] = jnp.zeros((LPAD - LENGTH, D), F32)

    local[4].wait()
    small_x.wait()
    s0 = smv[0].astype(F32)
    s1v = smv[1].astype(F32)
    for j, r in enumerate((G1, B1, OB, G2, B2, DB)):
        vec[j] = jnp.concatenate([s0[r : r + 1], s1v[r : r + 1]], axis=1)
    vec[6] = jnp.concatenate([s0[QV : QV + 1], s0[QV + 1 : QV + 2]], axis=1)
    vec[7] = jnp.zeros((1, D), F32)
    vec[8] = jnp.concatenate([s1v[QV : QV + 1], s1v[QV + 1 : QV + 2]], axis=1)
    vec[9] = jnp.concatenate([s0[UB : UB + 1], s0[UB + 1 : UB + 2]], axis=1)
    vec[10] = jnp.concatenate([s0[UB + 2 : UB + 3], s0[UB + 3 : UB + 4]], axis=1)
    vec[11] = jnp.concatenate([s1v[UB : UB + 1], s1v[UB + 1 : UB + 2]], axis=1)
    vec[12] = jnp.concatenate([s1v[UB + 2 : UB + 3], s1v[UB + 3 : UB + 4]], axis=1)

    def loop(n, body):
        def step(i, carry):
            body(i)
            return carry

        lax.fori_loop(0, n, step, 0)

    def transpose_into(src, k):
        def body(j):
            cols = ds(j * 128, 128)
            lt[k, cols, :] = src[:, cols].astype(F32).T.astype(BF16)

        loop(D // 128, body)

    def ln1(i):
        rows = ds(i * 96, 96)
        n, _ = norm_parts(xs[rows])
        h[rows] = (n * vec[0] + vec[1]).astype(BF16)

    loop(6, ln1)
    steps(0, 1)
    transpose_into(h, 0)
    steps(2, 3)
    rows_in[1].wait()
    for p in range(PAIRS):
        dys[p * LPAD : (p + 1) * LPAD] = jnp.concatenate(
            [cotv[p].astype(F32), jnp.zeros((LPAD - LENGTH, D), F32)], axis=0
        ).astype(BF16)
    steps(4, 6)

    def qkv_body(j, i):
        cols = ds(i * D + j * 256, 256)
        qkv[:, cols] = (dot(h[...], v0[:, cols]) + vec[6 + i, :, j * 256 : (j + 1) * 256]).astype(BF16)

    lane = lax.broadcasted_iota(jnp.int32, (1, 128), 1)
    low = lane < 64
    key = lax.broadcasted_iota(jnp.int32, (1, LPAD), 1)

    def attend(p, hp):
        rows = ds(p * LPAD, LPAD)
        q = qkv[rows, ds(hp * 128, 128)].astype(F32) * 0.125
        k = qkv[rows, ds(D + hp * 128, 128)]
        v = qkv[rows, ds(2 * D + hp * 128, 128)]
        valid = key < TEXT + counts[p]
        outs = []
        ls = lse[rows]
        for e in range(2):
            qm = jnp.where(low if e == 0 else jnp.logical_not(low), q, 0.0).astype(BF16)
            s = jnp.where(valid, dot_nt(qm, k), -1e30)
            m = jnp.max(s, axis=-1, keepdims=True)
            ex = jnp.exp(s - m)
            t = jnp.sum(ex, axis=-1, keepdims=True)
            ls = jnp.where(lane == 2 * hp + e, m + jnp.log(t), ls)
            outs.append(dot((ex * (1.0 / t)).astype(BF16), v))
        lse[rows] = ls
        o[rows, ds(hp * 128, 128)] = jnp.where(low, outs[0], outs[1]).astype(BF16)

    local[0].wait()
    for j in range(3):
        if j:
            step(6 + 3 * j)
        got(j)
        for i in range(3):
            qkv_body(j, i)

        def heads(i):
            for n in range(2):
                pl.when(i == n)(functools.partial(step, 7 + 3 * j + n))
            for p in range(PAIRS):
                attend(p, 2 * j + i)

        loop(2, heads)
    step(15)
    got(3)
    local[1].wait()

    def proj(i):
        cols = ds(i * 256, 256)
        x1[:, cols] = xs[:, cols] + dot(o[...], v1[:, cols]) + vec[2, :, cols]

    loop(3, proj)
    steps(16, 17)

    def ln2(i):
        rows = ds(i * 96, 96)
        n, _ = norm_parts(x1[rows])
        h[rows] = (n * vec[3] + vec[4]).astype(BF16)

    loop(6, ln2)
    step(18)
    for k in range(1, NZ):
        got_z(SHARED[0], k)
    got(4)
    local[2].wait()

    def up_tile(j):
        cols = ds(j * 256, 256)
        u = dot(h[...], v2[:, cols]) + vec[9 + j // 3, :, ds(lax.rem(j, 3) * 256, 256)]
        phi = 0.5 * (1.0 + lax.erf(u * 0.7071067811865476))
        gact[:, cols] = (u * phi).astype(BF16)
        dact[:, cols] = (phi + u * (0.3989422804014327 * jnp.exp(-0.5 * u * u))).astype(BF16)

    def down_chunk(i):
        par = lax.rem(i, 3)
        for x in range(2):
            cols = x * (FF // 2) + i * 256
            mine = gact[:, ds(cols + core * 128, 128)]
            other = gact[:, ds(cols + (1 - core) * 128, 128)]
            both = jnp.concatenate([mine, other], axis=1)
            for n in range(3):
                r = dot_tn(both, dys[:, n * 256 : (n + 1) * 256]).astype(BF16)
                ownd[par, x, :, n * 256 : (n + 1) * 256] = r[:128]
                sndd[par, x, :, n * 256 : (n + 1) * 256] = r[128:]
        c_copy(i, True).start()

    def phase_a(i):
        up_tile(i)
        for when, ns in ((0, (19,)), (1, (20, 21)), (2, (22,))):
            if ns[0] < STEPS:
                pl.when(i == when)(functools.partial(steps, ns[0], min(ns[-1], STEPS - 1)))
        for k in range(1, NZ):
            pl.when(i == k + 2)(functools.partial(got_z, SHARED[1], k))
        up_tile(6 + i)

        @pl.when(i > 1)
        def _():
            s1(i - 2, True)

        for when in range(2, 6):
            pl.when(i == when)(functools.partial(point, "A%d" % when))
        down_chunk(i)

    loop(6, phase_a)
    transpose_into(o, 1)
    transpose_into(h, 2)
    got(5)
    local[3].wait()

    def down_proj(n):
        cols = ds(n * 256, 256)
        r = (x1[:, cols] + dot(gact[...], v3[:, cols]) + vec[5, :, cols])
        for p in range(PAIRS):
            tokv[p, :, cols] = r[p * LPAD : p * LPAD + LENGTH].astype(BF16)

    loop(3, down_proj)
    result_out = pltpu.make_async_copy(tokv, res, lsem.at[5])
    result_out.start()
    s1(4, True)
    s1(5, True)
    point("B")

    def du_tile(j):
        cols = ds(j * 256, 256)
        du = (dot_nt(dys[...], v3[cols, :]) * dact[:, cols].astype(F32)).astype(BF16)
        dact[:, cols] = du
        sums = jnp.sum(du.astype(F32), axis=0, keepdims=True)
        for e in range(2):
            sacc[j // 6, 3 * UB + 2 * lax.rem(j, 6) + e] = sums[:, e * 128 : (e + 1) * 128]

    def col_chunk(i, j, sel, src):
        par = lax.rem(i, 3)
        for side, dst in ((core, own), (1 - core, snd)):
            u = 2 * j + side
            col_unit(dst, par, u, sel, src)
        c_copy(i, False).start()

    def col_unit(dst, par, u, sel, src):
        r = dot(lt[sel], src[:, ds(u * 256, 256)]).astype(BF16)
        dst[par, 0] = r[:HALF]
        dst[par, 1] = r[HALF:]

    def phase_c(j):
        du_tile(2 * j)
        du_tile(2 * j + 1)

        @pl.when(j > 1)
        def _():
            s1(4 + j, False)

        for when in range(6):
            pl.when(j == when)(functools.partial(point, "C%d" % when))
        col_chunk(6 + j, j, 2, dact)

    loop(6, phase_c)

    def dh2_tile(n):
        cols = ds(n * 256, 256)
        dh[:, cols] = dot_nt(dact[...], v2[cols, :])

    loop(3, dh2_tile)
    s1(10, False)
    s1(11, False)
    point("D")
    zero = jnp.zeros((1, D), F32)

    def spread(x, r, v):
        for j in range(v.shape[1] // 128):
            sacc[x, 3 * r + j] = v[:, j * 128 : (j + 1) * 128]

    def put(r, v):
        spread(0, r, v[:, :HALF])
        spread(1, r, v[:, HALF:])

    def ln2_back(i, carry):
        a, b, c2, d2 = carry
        rows = ds(i * 96, 96)
        n, r = norm_parts(x1[rows])
        g = dh[rows]
        e = g * vec[3]
        dy = dys[rows].astype(F32)
        dx = dy + r * (
            e - jnp.mean(e, axis=-1, keepdims=True) - n * jnp.mean(e * n, axis=-1, keepdims=True)
        )
        x1[rows] = dx
        da = dx.astype(BF16)
        qkv[rows, 3 * D :] = da
        return (
            a + jnp.sum(g * n, axis=0, keepdims=True),
            b + jnp.sum(g, axis=0, keepdims=True),
            c2 + jnp.sum(da.astype(F32), axis=0, keepdims=True),
            d2 + jnp.sum(dy, axis=0, keepdims=True),
        )

    sums = lax.fori_loop(0, 6, ln2_back, (zero, zero, zero, zero))
    for r, v in zip((G2, B2, OB, DB), sums):
        put(r, v)

    col_chunk(12, 5 + core // 2, 1, qkv)

    point("E0")

    def do_tile(n):
        cols = ds(n * 256, 256)
        o[:, cols] = dot_nt(qkv[:, 3 * D :], v1[cols, :]).astype(BF16)

    loop(3, do_tile)
    s1(12, False)
    point("E")

    def attend_back(i):
        for when in range(12):
            pl.when(i == when)(functools.partial(point, "F%d" % when))
        p = i // 6
        hp = lax.rem(i, 6)
        rows = ds(p * LPAD, LPAD)
        q = qkv[rows, ds(hp * 128, 128)]
        k = qkv[rows, ds(D + hp * 128, 128)]
        v = qkv[rows, ds(2 * D + hp * 128, 128)]
        g = o[rows, ds(hp * 128, 128)]
        qf = q.astype(F32) * 0.125
        gf = g.astype(F32)
        valid = key < TEXT + counts[p]
        ls = lse[rows]
        got3 = []
        for e in range(2):
            keep = low if e == 0 else jnp.logical_not(low)
            qm = jnp.where(keep, qf, 0.0).astype(BF16)
            gm = jnp.where(keep, gf, 0.0).astype(BF16)
            total = jnp.sum(jnp.where(lane == 2 * hp + e, ls, 0.0), axis=-1, keepdims=True)
            pr = jnp.where(valid, jnp.exp(dot_nt(qm, k) - total), 0.0)
            dp = dot_nt(gm, v)
            dsc = (pr * (dp - jnp.sum(pr * dp, axis=-1, keepdims=True))).astype(BF16)
            got3.append((dot(dsc, k), dot_tn(dsc, q), dot_tn(pr.astype(BF16), g)))
        for part, scale in ((0, 0.125), (1, 0.125), (2, 1.0)):
            r = jnp.where(low, got3[0][part], got3[1][part]) * scale
            qkv[rows, ds(part * D + hp * 128, 128)] = r.astype(BF16)

    loop(12, attend_back)

    def phase_g(t):
        @pl.when(t > 1)
        def _():
            s1(11 + t, False)

        for when in range(2, 4):
            pl.when(t == when)(functools.partial(point, "G%d" % when))
        col_chunk(13 + t, t, 0, qkv)

    loop(4, phase_g)
    for c in range(2):

        @pl.when(core == c)
        def _():
            for side, dst in ((c, own), (1 - c, snd)):
                col_unit(dst, 17 % 3, 8 + side, side, qkv)

    c_copy(17, False).start()
    s1(15, False)
    point("G4")

    def dh1_tile(n):
        cols = ds(n * 256, 256)
        dh[:, cols] = dot_nt(qkv[:, : 3 * D], v0[cols, :])

    loop(3, dh1_tile)
    s1(16, False)
    s1(17, False)
    point("H")

    def ln1_back(i, carry):
        a, b, qs, vs = carry
        rows = ds(i * 96, 96)
        n, r = norm_parts(xs[rows])
        g = dh[rows]
        e = g * vec[0]
        xs[rows] = x1[rows] + r * (
            e - jnp.mean(e, axis=-1, keepdims=True) - n * jnp.mean(e * n, axis=-1, keepdims=True)
        )
        return (
            a + jnp.sum(g * n, axis=0, keepdims=True),
            b + jnp.sum(g, axis=0, keepdims=True),
            qs + jnp.sum(qkv[rows, :D].astype(F32), axis=0, keepdims=True),
            vs + jnp.sum(qkv[rows, 2 * D : 3 * D].astype(F32), axis=0, keepdims=True),
        )

    ga, gb, qs, vs = lax.fori_loop(0, 6, ln1_back, (zero, zero, zero, zero))
    put(G1, ga)
    put(B1, gb)
    for x, v in ((0, qs), (1, vs)):
        spread(x, QV, v)
    for p in range(PAIRS):
        cotv[p] = xs[p * LPAD : p * LPAD + LENGTH].astype(BF16)
    grad_out = pltpu.make_async_copy(cotv, gtok, lsem.at[6])
    grad_out.start()
    point("I")

    n = POINTS[-1][2]
    for j, name in enumerate(("c", "x", "y")):
        cp = send(sacc, srecv.at[j], ssem.at[0, j], ssem.at[1, j], name)
        cp.start()
        for _ in range(2):
            point("Z%d" % n)
            n += 1
        cp.wait()
        sacc[...] = sacc[...] + srecv[j]
    copies = [
        send(sacc, srecv.at[3 + z], ssem.at[0, 2 + k], ssem.at[1, 2 + k], "z%d" % k) for k in range(1, NZ)
    ]
    for cp in copies:
        cp.start()
    srecv[3 + z] = sacc[...]
    for _ in range(2):
        point("Z%d" % n)
        n += 1
    for cp in copies:
        cp.wait()
    gsmall[...] = (srecv[3, f] + srecv[4, f]) + (srecv[5, f] + srecv[6, f])
    while n < SLOTS:
        point("Z%d" % n)
        n += 1
    result_out.wait()
    grad_out.wait()
    whole(acsem.at[0], 2304).wait_recv()
    for sem, rows in ((0, 864), (1, 864), (2, 2304), (3, 576)):
        whole(gsent.at[sem], rows).wait_send()
    for sem, rows in ((0, 2304), (1, 1152), (2, 864), (3, 864), (4, 1152), (5, 2304)):
        whole(rsent.at[sem], rows).wait_send()


def layer(*arrays):
    vm = pltpu.VMEM
    dma = pltpu.SemaphoreType.DMA
    any_ = pl.BlockSpec(memory_space=pl.ANY)
    inside = pl.BlockSpec(memory_space=pltpu.VMEM)
    pieces = len(PIECES)
    return pl.pallas_call(
        layer_kernel,
        out_shape=[
            jax.ShapeDtypeStruct((PAIRS, LENGTH, D), BF16),
            jax.ShapeDtypeStruct((PAIRS, LENGTH, D), BF16),
            jax.ShapeDtypeStruct((FF // 2, D), BF16),
            jax.ShapeDtypeStruct((HALF, FF), BF16),
            jax.ShapeDtypeStruct((HALF, FF), BF16),
            jax.ShapeDtypeStruct((36, 1, 128), F32),
        ],
        in_specs=[pl.BlockSpec(memory_space=pltpu.SMEM)] + [any_] * 7,
        out_specs=[any_] * 5 + [inside],
        scratch_shapes=[
            vm((PAIRS, LENGTH, D), BF16),
            vm((PAIRS, LENGTH, D), BF16),
            vm((ROWS, D), F32),
            vm((ROWS, D), BF16),
            vm((ROWS, D), BF16),
            vm((3, D, ROWS), BF16),
            vm((ROWS, 4 * D), BF16),
            vm((ROWS, D), BF16),
            vm((ROWS, 128), F32),
            vm((ROWS, D), F32),
            vm((ROWS, FF), BF16),
            vm((ROWS, FF), BF16),
            vm((ROWS, D), F32),
            vm((13, 1, D), F32),
            vm((2, 16, HALF), BF16),
            vm((D, 3 * D), BF16),
            vm((D, D), BF16),
            vm((D, FF), BF16),
            vm((FF, D), BF16),
            vm((3, 2, HALF, 256), BF16),
            vm((3, 2, HALF, 256), BF16),
            vm((3, 2, 128, D), BF16),
            vm((3, 2, 128, D), BF16),
            vm((12, 2, HALF, 256), BF16),
            vm((12, HALF, 256), BF16),
            vm((12, HALF // 2, 256), BF16),
            vm((12, NZ - 1, HALF // 8, 256), BF16),
            vm((12, HALF // 8, 256), BF16),
            vm((6, 2, 128, D), BF16),
            vm((6, 128, D), BF16),
            vm((6, 64, D), BF16),
            vm((6, NZ - 1, 16, D), BF16),
            vm((6, 16, D), BF16),
            vm((2, 36, 1, 128), F32),
            vm((7, 2, 36, 1, 128), F32),
            dma((pieces,)),
            dma((pieces,)),
            dma((6,)),
            dma((len(SHARED), NZ - 1, 2)),
            dma((4,)),
            dma((7,)),
            dma((6,)),
            dma((6,)),
            dma((NCH,)),
            dma((2 * NCH,)),
            dma((NCH,)),
            dma((NCH,)),
            dma((NCH,)),
            dma((NCH,)),
            dma((1,)),
            dma((NCH,)),
            dma((2, 7)),
        ],
        compiler_params=pltpu.CompilerParams(
            collective_id=1, has_side_effects=True, vmem_limit_bytes=63 << 20
        ),
        name="layer",
    )(*arrays)


def finish_kernel(gdown, gup, gqo, gsmall, res, gtok, down, up, qkv, out, res_out, gtok_out, *vectors):
    down[...] = gdown[...].astype(F32)
    up[...] = gup[...].astype(F32)
    qkv[...] = gqo[:, : 3 * D].astype(F32)
    out[...] = gqo[:, 3 * D :].astype(F32)
    res_out[...] = res[...]
    gtok_out[...] = gtok[...]

    @pl.when(pl.program_id(0) == 0)
    def _():
        at = 0
        for v in vectors:
            n = v.shape[0] // 128
            for j in range(n):
                v[j * 128 : (j + 1) * 128] = gsmall[at + j, 0]
            at += n


def finish(gdown, gup, gqo, gsmall, res, gtok):
    steps = 8
    rows = PAIRS * LENGTH // 7

    def cut(n, width):
        return pl.BlockSpec((n, width), lambda i: (i, 0))

    tokens = pl.BlockSpec((rows, D), lambda i: (jnp.minimum(i, 6), 0))
    out = pl.pallas_call(
        finish_kernel,
        grid=(steps,),
        out_shape=[
            jax.ShapeDtypeStruct((FF // 2, D), F32),
            jax.ShapeDtypeStruct((HALF, FF), F32),
            jax.ShapeDtypeStruct((HALF, 3 * D), F32),
            jax.ShapeDtypeStruct((HALF, D), F32),
            jax.ShapeDtypeStruct((PAIRS * LENGTH, D), BF16),
            jax.ShapeDtypeStruct((PAIRS * LENGTH, D), BF16),
        ]
        + [jax.ShapeDtypeStruct((n * HALF,), F32) for n in SMALL],
        in_specs=[
            cut(FF // 2 // steps, D),
            cut(HALF // steps, FF),
            cut(HALF // steps, FF),
            pl.BlockSpec((36, 1, 128), lambda i: (0, 0, 0)),
            tokens,
            tokens,
        ],
        out_specs=[
            cut(FF // 2 // steps, D),
            cut(HALF // steps, FF),
            cut(HALF // steps, 3 * D),
            cut(HALF // steps, D),
            tokens,
            tokens,
        ]
        + [pl.BlockSpec((n * HALF,), lambda i: (0,)) for n in SMALL],
        name="finish",
    )(gdown, gup, gqo, gsmall, res.reshape(PAIRS * LENGTH, D), gtok.reshape(PAIRS * LENGTH, D))
    return out


def on_device(extra, tokens, patch_counts, cotangent, norm1_gain, norm1_bias, qkv_weight, qv_bias,
              out_weight, out_bias, norm2_gain, norm2_bias, up_weight, up_bias, down_weight, down_bias):
    small, at = 0, 0
    for v in (norm1_gain, norm1_bias, qv_bias, out_bias, norm2_gain, norm2_bias, up_bias, down_bias):
        small = small + jnp.pad(v, (at, 16 * HALF - at - v.size))
        at += v.size
    small = small.reshape(16, HALF)
    result, grad_tokens, gdown, gup, gqo, gsmall = layer(
        patch_counts, tokens, cotangent, qkv_weight, out_weight, up_weight, down_weight, small
    )
    down, up, qkv, out, result, grad_tokens, *parts = finish(gdown, gup, gqo, gsmall, result, grad_tokens)
    grads = [down, up, qkv, out] + parts
    if extra is not None:
        grads = lax.psum(grads, "dp", axis_index_groups=extra)
    down, up, qkv, out, *parts = grads
    result, grad_tokens = (v.reshape(PAIRS, LENGTH, D) for v in (result, grad_tokens))
    return (
        result, grad_tokens, parts[0], parts[1], qkv, parts[2], out, parts[3],
        parts[4], parts[5], up, parts[6], down, parts[7],
    )


def solution(mesh):
    dp = mesh.shape["dp"]
    extra = None
    if dp > GROUP:
        extra = [[j + GROUP * i for i in range(dp // GROUP)] for j in range(GROUP)]
    row = P(("dp", "fsdp"), None, None)
    vec = P("fsdp")
    mat = P("fsdp", None)
    return jax.shard_map(
        functools.partial(on_device, extra),
        mesh=mesh,
        in_specs=(row, P(("dp", "fsdp")), row, vec, vec, mat, vec, mat, vec, vec, vec, mat, vec, mat, vec),
        out_specs=(row, row, vec, vec, mat, vec, mat, vec, vec, vec, mat, vec, mat, vec),
        check_vma=False,
    )
```

```python
import functools

import jax
import jax.numpy as jnp
from jax import lax
from jax.experimental import pallas as pl
from jax.experimental.pallas import tpu as pltpu
from jax.sharding import PartitionSpec as P

TEXT = 40
MESH = pl.DeviceIdType.MESH
BF16 = jnp.bfloat16
F32 = jnp.float32
EPS = 1e-06
NZ = 4
GROUP = 16
PAIRS = 2
LENGTH = 280
LPAD = 288
ROWS = PAIRS * LPAD
D = 768
FF = 3072
HALF = D // 2
NCH = 18
SPLIT = 18
PARTS = [(i, 0, None) for i in range(SPLIT)] + [(i, 128 * e, 128) for i in range(SPLIT, NCH) for e in range(2)]
NP = len(PARTS)
GW = 5
PIECES = (
    [(2, 4, 0, 96, FF // 2, FF // 8, 0, FF // 8)]
    + [(0, j, 0, 96, k * D + j * 256, 256, 0, 0) for j in range(3) for k in range(3)]
    + [(1, 3, 48 * j, 48, 0, D, 0, 0) for j in range(2)]
    + [(2, 4, 0, 96, 384 * j, 384, 0, 0) for j in range(4)]
    + [(3, 5, 0, 48, 0, D, 48, 0)]
    + [(3, 5, 192 + 96 * j, 96, 0, D, 0, 0) for j in range(2)]
)
SHARED = [g for g, p in enumerate(PIECES) if p[6] or p[7]]
GLAG = 3
STEPS = len(PIECES) + GLAG
SMALL = (1, 1, 2, 1, 1, 1, 4, 1)
G1, B1, QV, OB, G2, B2, UB, DB = 0, 1, 2, 4, 5, 6, 7, 11


def plan():
    points = list(POINTS)
    points += [("Z%d" % n, NCH, n + 1) for n in range(points[-1][2], SLOTS)]
    acts, done, started = {}, 0, 0
    for name, ready, upto in points:
        todo = acts[name] = []
        while True:
            ahead = AHEAD if done < NARROW else AHEAD_LAST
            while started < min(2 * NP, 2 * BY[ready], done + ahead):
                todo.append(("start", started))
                started += 1
            if done == upto:
                break
            assert done >= 2 * NP or started > done
            todo.append(("slot", done))
            done += 1
    return acts


POINTS = (
    ("A1", 1, 0), ("A2", 1, 0), ("A3", 2, 1), ("A4", 3, 2), ("A5", 4, 3), ("B", 6, 5), ("C0", 6, 6), ("C1", 6,
    8), ("C2", 7, 9), ("C3", 8, 10), ("C4", 9, 11), ("C5", 10, 13), ("D", 12, 14), ("E0", 12, 15), ("E", 13,
    17), ("F0", 13, 17), ("F1", 13, 17), ("F2", 13, 18), ("F3", 13, 18), ("F4", 13, 19), ("F5", 13, 20),
    ("F6", 13, 20), ("F7", 13, 21), ("F8", 13, 22), ("F9", 13, 22), ("F10", 13, 23), ("F11", 13, 24), ("G2",
    14, 25), ("G3", 15, 26), ("G4", 16, 26), ("H", 18, 27), ("I", 18, 29),
)
SLOTS = 2 * NP + 11
BY = [sum(p[0] < n for p in PARTS) for n in range(NCH + 1)]
AHEAD, AHEAD_LAST, NARROW = 4, 4, 24
PLAN = plan()


def dot(a, b):
    return jnp.dot(a, b, preferred_element_type=F32)


def dot_nt(a, b):
    return lax.dot_general(a, b, (((1,), (1,)), ((), ())), preferred_element_type=F32)


def dot_tn(a, b):
    return lax.dot_general(a, b, (((0,), (0,)), ((), ())), preferred_element_type=F32)


def mult(x, n):
    return x if isinstance(x, int) else pl.multiple_of(x, n)


def ds(start, size, n=None):
    return pl.ds(mult(start, n or size), size)


def places():
    d = lax.axis_index("dp")
    f = lax.axis_index("fsdp")
    core = lax.rem(d, 2)
    y = lax.rem(d // 2, 2)
    z = lax.rem(d // 4, NZ)
    base = d - lax.rem(d, GROUP)

    def at(zz, yy, cc):
        return base + zz * 4 + yy * 2 + cc

    peers = {
        "c": (at(z, y, 1 - core), f),
        "x": (d, 1 - f),
        "y": (at(z, 1 - y, core), f),
    }
    for k in range(1, NZ):
        peers["z%d" % k] = (at(lax.rem(z + k, NZ), y, core), f)
    return f, core, y, z, peers


def norm_parts(v):
    c = v - jnp.mean(v, axis=-1, keepdims=True)
    r = lax.rsqrt(jnp.mean(c * c, axis=-1, keepdims=True) + EPS)
    return c * r, r


def layer_kernel(
    counts, tok, cot, w0, w1, w2, w3, s_in,
    res, gtok, gdown, gup, gqo, gsmall,
    tokv, cotv, xs, dys, h, lt, qkv, o, lse, x1, gact, dact, dh, vec, smv,
    v0, v1, v2, v3,
    own, snd, ownd, sndd,
    cb, xb, yb, zb, stg, cbd, xbd, ybd, zbd, stgd, sacc, srecv,
    gxs, gys, gcs, gzs, gsent, lsem, csent, rsent, csem, xsem, ysem, zsem, azsem, aysem, acsem, psem, ssem,
):
    f, core, y, z, peers = places()
    ins = (w0, w1, w2, w3)
    ws = (v0, v1, v2, v3)
    barrier = pltpu.get_barrier_semaphore()
    for name in peers:
        pl.semaphore_signal(barrier, inc=1, device_id=peers[name], device_id_type=MESH)

    def send(src, dst, sent, arrived, name):
        return pltpu.make_async_remote_copy(
            src_ref=src, dst_ref=dst, send_sem=sent, recv_sem=arrived,
            device_id=peers[name], device_id_type=MESH,
        )

    def piece(g, half, yy, zz=None):
        w, _, r0, rows, c0, cols, zr, zc = PIECES[g]
        full = ins[w].shape[0]
        zz = z if zz is None else zz
        start = half * full + (core * 2 + yy) * (full // 4) + r0 + zz * zr
        return w, (pl.ds(pl.multiple_of(start, 16), rows), ds(c0 + zz * zc, cols, 128))

    def same(g, yy, zz, sent, arrived, name):
        w, at = piece(g, 1 - f, yy, zz)
        return send(ws[w].at[at], ws[w].at[at], sent, arrived, name)

    def gx(g):
        w, there = piece(g, f, y)
        _, here = piece(g, 0, y)
        return send(ins[w].at[here], ws[w].at[there], gsent.at[0], gxs.at[g], "x")

    def gy(g):
        return same(g, y, z, gsent.at[1], gys.at[g], "y")

    def gc(g, e, k=0):
        arrived = gcs.at[PIECES[g][1]]
        return same(g, y if e == 0 else 1 - y, lax.rem(z + NZ - k, NZ), gsent.at[2], arrived, "c")

    def gz(g, e, k):
        return same(g, y if e == 0 else 1 - y, z, gsent.at[3], gzs.at[SHARED.index(g), k - 1, e], "z%d" % k)

    def got_x(g):
        gx(g).wait_recv()
        if g + GW < len(PIECES):
            gx(g + GW).start()
        gy(g).start()
        gc(g, 0).start()
        if g in SHARED:
            for k in range(1, NZ):
                gz(g, 0, k).start()

    def got_y(g):
        gy(g).wait_recv()
        gc(g, 1).start()
        if g in SHARED:
            for k in range(1, NZ):
                gz(g, 1, k).start()

    def step(n):
        if n < len(PIECES):
            got_x(n)
        if n >= GLAG:
            got_y(n - GLAG)

    def steps(first, last):
        for n in range(first, last + 1):
            step(n)

    def got_z(g, k):
        for e in range(2):
            gz(g, e, k).wait_recv()
            gc(g, e, k).start()

    def whole(sem, rows):
        at = v3.at[pl.ds(0, rows)]
        return send(at, at, sem, sem, "c")

    def got(j):
        whole(gcs.at[j], (192, 192, 192, 192, 768, 768)[j]).wait_recv()

    rows_in = (pltpu.make_async_copy(tok, tokv, lsem.at[5]), pltpu.make_async_copy(cot, cotv, lsem.at[6]))
    rows_in[0].start()
    local = []
    for i in range(4):
        full = ins[i].shape[0]
        local.append(pltpu.make_async_copy(ins[i], ws[i].at[pl.ds(pl.multiple_of(f * full, 16), full)], lsem.at[i]))
    local.append(pltpu.make_async_copy(s_in, smv.at[f], lsem.at[4]))
    local[4].start()
    pl.semaphore_wait(barrier, len(peers))
    small_x = send(s_in, smv.at[f], ssem.at[0, 6], ssem.at[1, 6], "x")
    small_x.start()
    for g in range(GW):
        gx(g).start()
    rows_in[1].start()
    for i in range(4):
        local[i].start()

    def c_copy(i, down):
        if down:
            return send(sndd.at[lax.rem(i, 3)], cbd.at[i], csent.at[lax.rem(i, 3)], csem.at[i], "c")
        return send(snd.at[lax.rem(i, 3)], cb.at[i - 6], csent.at[3 + lax.rem(i, 3)], csem.at[i], "c")

    def bufs(i):
        if i < 6:
            return i, 128, D, cbd, xbd, ybd, zbd, stgd
        return i - 6, HALF, 256, cb, xb, yb, zb, stg

    def bufs(n):
        i, c0, width = PARTS[n]
        if i < 6:
            j, ur, refs = i, 128, (cbd, xbd, ybd, zbd, stgd)
        else:
            j, ur, refs = i - 6, HALF, (cb, xb, yb, zb, stg)
        if width is None:
            return (ur,) + tuple(r.at[j] for r in refs)
        at = pl.ds(c0, width)
        cc, xx, yy, zz, st = refs
        return ur, cc.at[j, :, :, at], xx.at[j, :, at], yy.at[j, :, at], zz.at[j, :, :, at], st.at[j, :, at]

    def x_copy(h):
        n, e = h // 2, h % 2
        ur, cc, xx, _, _, _ = bufs(n)
        half = ds(((1 - y) if e == 0 else y) * (ur // 2), ur // 2)
        return send(cc.at[1 - f, half], xx.at[half], rsent.at[0], xsem.at[h], "x")

    def y_copy(n):
        ur, _, xx, yy, _, _ = bufs(n)
        return send(xx.at[ds((1 - y) * (ur // 2), ur // 2)], yy, rsent.at[1], ysem.at[n], "y")

    def z_copy(n, k):
        ur, _, _, yy, zz, _ = bufs(n)
        return send(
            yy.at[ds(lax.rem(z + k, NZ) * (ur // 8), ur // 8)], zz.at[k - 1], rsent.at[2], zsem.at[n], "z%d" % k
        )

    def outpart(n, start, rows):
        i, c0, width = PARTS[n]
        j = i % 6 if i < 12 else (i - 12 + 5) % 6
        if i < 6:
            return gdown.at[pl.ds(pl.multiple_of((2 * j + core) * 128 + start, 16), rows), :]
        ref = gup if i < 12 else gqo
        return ref.at[pl.ds(mult(start, 16), rows), ds((2 * j + core) * 256 + c0, width or 256, 128)]

    def own_piece(n):
        ur, _, _, _, _, st = bufs(n)
        return outpart(n, y * (ur // 2) + z * (ur // 8), ur // 8), st

    def p_copy(n):
        dst, src = own_piece(n)
        return pltpu.make_async_copy(src, dst, psem.at[n])

    def az_copy(n, k):
        dst, src = own_piece(n)
        return send(src, dst, rsent.at[3], azsem.at[n], "z%d" % k)

    def ay_copy(n):
        ur = bufs(n)[0]
        part = outpart(n, y * (ur // 2), ur // 2)
        return send(part, part, rsent.at[4], aysem.at[n], "y")

    def ac_copy(n):
        part = outpart(n, 0, bufs(n)[0])
        return send(part, part, rsent.at[5], acsem.at[0], "c")

    def s1(i, down):
        c_copy(i, down).wait()
        if down:
            cbd[i] = (cbd[i].astype(F32) + ownd[lax.rem(i, 3)].astype(F32)).astype(BF16)
        else:
            cb[i - 6] = (cb[i - 6].astype(F32) + own[lax.rem(i, 3)].astype(F32)).astype(BF16)

    def s2(h):
        x_copy(h).wait_recv()
        n = h // 2
        if h % 2 == 0:
            ur, cc, xx, _, _, _ = bufs(n)
            half = ds((1 - y) * (ur // 2), ur // 2)
            xx[half] = (xx[half].astype(F32) + cc[f, half].astype(F32)).astype(BF16)
            y_copy(n).start()

    def s3(n):
        y_copy(n).wait_recv()
        ur, cc, xx, yy, _, _ = bufs(n)
        half = ds(y * (ur // 2), ur // 2)
        yy[...] = (yy[...].astype(F32) + (xx[half].astype(F32) + cc[f, half].astype(F32))).astype(BF16)
        for k in range(1, NZ):
            z_copy(n, k).start()

    def s4(n):
        ur, _, _, yy, zz, st = bufs(n)
        send(zz, zz, rsent.at[2], zsem.at[n], "z1").wait_recv()
        total = yy[ds(z * (ur // 8), ur // 8)].astype(F32)
        for k in range(1, NZ):
            total = total + zz[k - 1].astype(F32)
        st[...] = total.astype(BF16)
        p_copy(n).start()
        for k in range(1, NZ):
            az_copy(n, k).start()

    def s5(n):
        p_copy(n).wait()
        zz = bufs(n)[4]
        send(zz, zz, rsent.at[3], azsem.at[n], "z1").wait_recv()
        ay_copy(n).start()

    def s6(n):
        ay_copy(n).wait_recv()
        ac_copy(n).start()

    def slot(n):
        if n < 2 * NP:
            s2(n)
        for lag, stage in ((3, s3), (6, s4), (9, s5), (12, s6)):
            if (n - lag) % 2 == 0 and 0 <= (n - lag) // 2 < NP:
                stage((n - lag) // 2)

    def point(name):
        for what, n in PLAN[name]:
            if what == "start":
                x_copy(n).start()
            else:
                slot(n)

    rows_in[0].wait()
    for p in range(PAIRS):
        xs[p * LPAD : p * LPAD + LENGTH] = tokv[p].astype(F32)
        xs[p * LPAD + LENGTH : (p + 1) * LPAD] = jnp.zeros((LPAD - LENGTH, D), F32)

    local[4].wait()
    small_x.wait()
    s0 = smv[0].astype(F32)
    s1v = smv[1].astype(F32)
    for j, r in enumerate((G1, B1, OB, G2, B2, DB)):
        vec[j] = jnp.concatenate([s0[r : r + 1], s1v[r : r + 1]], axis=1)
    vec[6] = jnp.concatenate([s0[QV : QV + 1], s0[QV + 1 : QV + 2]], axis=1)
    vec[7] = jnp.zeros((1, D), F32)
    vec[8] = jnp.concatenate([s1v[QV : QV + 1], s1v[QV + 1 : QV + 2]], axis=1)
    vec[9] = jnp.concatenate([s0[UB : UB + 1], s0[UB + 1 : UB + 2]], axis=1)
    vec[10] = jnp.concatenate([s0[UB + 2 : UB + 3], s0[UB + 3 : UB + 4]], axis=1)
    vec[11] = jnp.concatenate([s1v[UB : UB + 1], s1v[UB + 1 : UB + 2]], axis=1)
    vec[12] = jnp.concatenate([s1v[UB + 2 : UB + 3], s1v[UB + 3 : UB + 4]], axis=1)

    def loop(n, body):
        def step(i, carry):
            body(i)
            return carry

        lax.fori_loop(0, n, step, 0)

    def transpose_into(src, k):
        def body(j):
            cols = ds(j * 128, 128)
            lt[k, cols, :] = src[:, cols].astype(F32).T.astype(BF16)

        loop(D // 128, body)

    def ln1(i):
        rows = ds(i * 96, 96)
        n, _ = norm_parts(xs[rows])
        h[rows] = (n * vec[0] + vec[1]).astype(BF16)

    loop(6, ln1)
    steps(0, 1)
    transpose_into(h, 0)
    steps(2, 3)
    rows_in[1].wait()
    for p in range(PAIRS):
        dys[p * LPAD : (p + 1) * LPAD] = jnp.concatenate(
            [cotv[p].astype(F32), jnp.zeros((LPAD - LENGTH, D), F32)], axis=0
        ).astype(BF16)
    steps(4, 6)

    def qkv_body(j, i):
        cols = ds(i * D + j * 256, 256)
        qkv[:, cols] = (dot(h[...], v0[:, cols]) + vec[6 + i, :, j * 256 : (j + 1) * 256]).astype(BF16)

    lane = lax.broadcasted_iota(jnp.int32, (1, 128), 1)
    low = lane < 64
    key = lax.broadcasted_iota(jnp.int32, (1, LPAD), 1)

    def attend(p, hp):
        rows = ds(p * LPAD, LPAD)
        q = qkv[rows, ds(hp * 128, 128)].astype(F32) * 0.125
        k = qkv[rows, ds(D + hp * 128, 128)]
        v = qkv[rows, ds(2 * D + hp * 128, 128)]
        valid = key < TEXT + counts[p]
        outs = []
        ls = lse[rows]
        for e in range(2):
            qm = jnp.where(low if e == 0 else jnp.logical_not(low), q, 0.0).astype(BF16)
            s = jnp.where(valid, dot_nt(qm, k), -1e30)
            m = jnp.max(s, axis=-1, keepdims=True)
            ex = jnp.exp(s - m)
            t = jnp.sum(ex, axis=-1, keepdims=True)
            ls = jnp.where(lane == 2 * hp + e, m + jnp.log(t), ls)
            outs.append(dot((ex * (1.0 / t)).astype(BF16), v))
        lse[rows] = ls
        o[rows, ds(hp * 128, 128)] = jnp.where(low, outs[0], outs[1]).astype(BF16)

    local[0].wait()
    for j in range(3):
        if j:
            step(6 + 3 * j)
        got(j)
        for i in range(3):
            qkv_body(j, i)

        def heads(i):
            for n in range(2):
                pl.when(i == n)(functools.partial(step, 7 + 3 * j + n))
            for p in range(PAIRS):
                attend(p, 2 * j + i)

        loop(2, heads)
    step(15)
    got(3)
    local[1].wait()

    def proj(i):
        cols = ds(i * 256, 256)
        x1[:, cols] = xs[:, cols] + dot(o[...], v1[:, cols]) + vec[2, :, cols]

    loop(3, proj)
    steps(16, 17)

    def ln2(i):
        rows = ds(i * 96, 96)
        n, _ = norm_parts(x1[rows])
        h[rows] = (n * vec[3] + vec[4]).astype(BF16)

    loop(6, ln2)
    step(18)
    for k in range(1, NZ):
        got_z(SHARED[0], k)
    got(4)
    local[2].wait()

    def up_tile(j):
        cols = ds(j * 256, 256)
        u = dot(h[...], v2[:, cols]) + vec[9 + j // 3, :, ds(lax.rem(j, 3) * 256, 256)]
        phi = 0.5 * (1.0 + lax.erf(u * 0.7071067811865476))
        gact[:, cols] = (u * phi).astype(BF16)
        dact[:, cols] = (phi + u * (0.3989422804014327 * jnp.exp(-0.5 * u * u))).astype(BF16)

    def down_chunk(i):
        par = lax.rem(i, 3)
        for x in range(2):
            cols = x * (FF // 2) + i * 256
            mine = gact[:, ds(cols + core * 128, 128)]
            other = gact[:, ds(cols + (1 - core) * 128, 128)]
            both = jnp.concatenate([mine, other], axis=1)
            for n in range(3):
                r = dot_tn(both, dys[:, n * 256 : (n + 1) * 256]).astype(BF16)
                ownd[par, x, :, n * 256 : (n + 1) * 256] = r[:128]
                sndd[par, x, :, n * 256 : (n + 1) * 256] = r[128:]
        c_copy(i, True).start()

    def phase_a(i):
        up_tile(i)
        for when, ns in ((0, (19,)), (1, (20, 21)), (2, (22,))):
            if ns[0] < STEPS:
                pl.when(i == when)(functools.partial(steps, ns[0], min(ns[-1], STEPS - 1)))
        for k in range(1, NZ):
            pl.when(i == k + 2)(functools.partial(got_z, SHARED[1], k))
        up_tile(6 + i)

        @pl.when(i == 1)
        def _():
            s1(0, True)

        @pl.when(i > 2)
        def _():
            s1(i - 2, True)

        for when in range(1, 6):
            pl.when(i == when)(functools.partial(point, "A%d" % when))
        down_chunk(i)

    loop(6, phase_a)
    transpose_into(o, 1)
    transpose_into(h, 2)
    got(5)
    local[3].wait()

    def down_proj(n):
        cols = ds(n * 256, 256)
        r = (x1[:, cols] + dot(gact[...], v3[:, cols]) + vec[5, :, cols])
        for p in range(PAIRS):
            tokv[p, :, cols] = r[p * LPAD : p * LPAD + LENGTH].astype(BF16)

    loop(3, down_proj)
    result_out = pltpu.make_async_copy(tokv, res, lsem.at[5])
    result_out.start()
    s1(4, True)
    s1(5, True)
    point("B")

    def du_tile(j):
        cols = ds(j * 256, 256)
        du = (dot_nt(dys[...], v3[cols, :]) * dact[:, cols].astype(F32)).astype(BF16)
        dact[:, cols] = du
        sums = jnp.sum(du.astype(F32), axis=0, keepdims=True)
        for e in range(2):
            sacc[j // 6, 3 * UB + 2 * lax.rem(j, 6) + e] = sums[:, e * 128 : (e + 1) * 128]

    def col_chunk(i, j, sel, src):
        par = lax.rem(i, 3)
        for side, dst in ((core, own), (1 - core, snd)):
            u = 2 * j + side
            col_unit(dst, par, u, sel, src)
        c_copy(i, False).start()

    def col_unit(dst, par, u, sel, src):
        r = dot(lt[sel], src[:, ds(u * 256, 256)]).astype(BF16)
        dst[par, 0] = r[:HALF]
        dst[par, 1] = r[HALF:]

    def phase_c(j):
        du_tile(2 * j)
        du_tile(2 * j + 1)

        @pl.when(j > 1)
        def _():
            s1(4 + j, False)

        for when in range(6):
            pl.when(j == when)(functools.partial(point, "C%d" % when))
        col_chunk(6 + j, j, 2, dact)

    loop(6, phase_c)

    def dh2_tile(n):
        cols = ds(n * 256, 256)
        dh[:, cols] = dot_nt(dact[...], v2[cols, :])

    loop(3, dh2_tile)
    s1(10, False)
    s1(11, False)
    point("D")
    zero = jnp.zeros((1, D), F32)

    def spread(x, r, v):
        for j in range(v.shape[1] // 128):
            sacc[x, 3 * r + j] = v[:, j * 128 : (j + 1) * 128]

    def put(r, v):
        spread(0, r, v[:, :HALF])
        spread(1, r, v[:, HALF:])

    def ln2_back(i, carry):
        a, b, c2, d2 = carry
        rows = ds(i * 96, 96)
        n, r = norm_parts(x1[rows])
        g = dh[rows]
        e = g * vec[3]
        dy = dys[rows].astype(F32)
        dx = dy + r * (
            e - jnp.mean(e, axis=-1, keepdims=True) - n * jnp.mean(e * n, axis=-1, keepdims=True)
        )
        x1[rows] = dx
        da = dx.astype(BF16)
        qkv[rows, 3 * D :] = da
        return (
            a + jnp.sum(g * n, axis=0, keepdims=True),
            b + jnp.sum(g, axis=0, keepdims=True),
            c2 + jnp.sum(da.astype(F32), axis=0, keepdims=True),
            d2 + jnp.sum(dy, axis=0, keepdims=True),
        )

    sums = lax.fori_loop(0, 6, ln2_back, (zero, zero, zero, zero))
    for r, v in zip((G2, B2, OB, DB), sums):
        put(r, v)

    col_chunk(12, 5 + core // 2, 1, qkv)

    point("E0")

    def do_tile(n):
        cols = ds(n * 256, 256)
        o[:, cols] = dot_nt(qkv[:, 3 * D :], v1[cols, :]).astype(BF16)

    loop(3, do_tile)
    s1(12, False)
    point("E")

    def attend_back(i):
        for when in range(12):
            pl.when(i == when)(functools.partial(point, "F%d" % when))
        p = i // 6
        hp = lax.rem(i, 6)
        rows = ds(p * LPAD, LPAD)
        q = qkv[rows, ds(hp * 128, 128)]
        k = qkv[rows, ds(D + hp * 128, 128)]
        v = qkv[rows, ds(2 * D + hp * 128, 128)]
        g = o[rows, ds(hp * 128, 128)]
        qf = q.astype(F32) * 0.125
        gf = g.astype(F32)
        valid = key < TEXT + counts[p]
        ls = lse[rows]
        got3 = []
        for e in range(2):
            keep = low if e == 0 else jnp.logical_not(low)
            qm = jnp.where(keep, qf, 0.0).astype(BF16)
            gm = jnp.where(keep, gf, 0.0).astype(BF16)
            total = jnp.sum(jnp.where(lane == 2 * hp + e, ls, 0.0), axis=-1, keepdims=True)
            pr = jnp.where(valid, jnp.exp(dot_nt(qm, k) - total), 0.0)
            dp = dot_nt(gm, v)
            dsc = (pr * (dp - jnp.sum(pr * dp, axis=-1, keepdims=True))).astype(BF16)
            got3.append((dot(dsc, k), dot_tn(dsc, q), dot_tn(pr.astype(BF16), g)))
        for part, scale in ((0, 0.125), (1, 0.125), (2, 1.0)):
            r = jnp.where(low, got3[0][part], got3[1][part]) * scale
            qkv[rows, ds(part * D + hp * 128, 128)] = r.astype(BF16)

    loop(12, attend_back)

    def phase_g(t):
        @pl.when(t > 1)
        def _():
            s1(11 + t, False)

        for when in range(2, 4):
            pl.when(t == when)(functools.partial(point, "G%d" % when))
        col_chunk(13 + t, t, 0, qkv)

    loop(4, phase_g)
    for c in range(2):

        @pl.when(core == c)
        def _():
            for side, dst in ((c, own), (1 - c, snd)):
                col_unit(dst, 17 % 3, 8 + side, side, qkv)

    c_copy(17, False).start()
    s1(15, False)
    point("G4")

    def dh1_tile(n):
        cols = ds(n * 256, 256)
        dh[:, cols] = dot_nt(qkv[:, : 3 * D], v0[cols, :])

    loop(3, dh1_tile)
    s1(16, False)
    s1(17, False)
    point("H")

    def ln1_back(i, carry):
        a, b, qs, vs = carry
        rows = ds(i * 96, 96)
        n, r = norm_parts(xs[rows])
        g = dh[rows]
        e = g * vec[0]
        xs[rows] = x1[rows] + r * (
            e - jnp.mean(e, axis=-1, keepdims=True) - n * jnp.mean(e * n, axis=-1, keepdims=True)
        )
        return (
            a + jnp.sum(g * n, axis=0, keepdims=True),
            b + jnp.sum(g, axis=0, keepdims=True),
            qs + jnp.sum(qkv[rows, :D].astype(F32), axis=0, keepdims=True),
            vs + jnp.sum(qkv[rows, 2 * D : 3 * D].astype(F32), axis=0, keepdims=True),
        )

    ga, gb, qs, vs = lax.fori_loop(0, 6, ln1_back, (zero, zero, zero, zero))
    put(G1, ga)
    put(B1, gb)
    for x, v in ((0, qs), (1, vs)):
        spread(x, QV, v)
    for p in range(PAIRS):
        cotv[p] = xs[p * LPAD : p * LPAD + LENGTH].astype(BF16)
    grad_out = pltpu.make_async_copy(cotv, gtok, lsem.at[6])
    grad_out.start()
    point("I")

    n = POINTS[-1][2]
    for j, name in enumerate(("c", "x", "y")):
        cp = send(sacc, srecv.at[j], ssem.at[0, j], ssem.at[1, j], name)
        cp.start()
        for _ in range(2):
            point("Z%d" % n)
            n += 1
        cp.wait()
        sacc[...] = sacc[...] + srecv[j]
    copies = [
        send(sacc, srecv.at[3 + z], ssem.at[0, 2 + k], ssem.at[1, 2 + k], "z%d" % k) for k in range(1, NZ)
    ]
    for cp in copies:
        cp.start()
    srecv[3 + z] = sacc[...]
    for _ in range(2):
        point("Z%d" % n)
        n += 1
    for cp in copies:
        cp.wait()
    gsmall[...] = (srecv[3, f] + srecv[4, f]) + (srecv[5, f] + srecv[6, f])
    while n < SLOTS:
        point("Z%d" % n)
        n += 1
    result_out.wait()
    grad_out.wait()
    whole(acsem.at[0], 2304).wait_recv()
    for sem, rows in ((0, 864), (1, 864), (2, 2304), (3, 576)):
        whole(gsent.at[sem], rows).wait_send()
    for sem, rows in ((0, 2304), (1, 1152), (2, 864), (3, 864), (4, 1152), (5, 2304)):
        whole(rsent.at[sem], rows).wait_send()


def layer(*arrays):
    vm = pltpu.VMEM
    dma = pltpu.SemaphoreType.DMA
    any_ = pl.BlockSpec(memory_space=pl.ANY)
    inside = pl.BlockSpec(memory_space=pltpu.VMEM)
    pieces = len(PIECES)
    return pl.pallas_call(
        layer_kernel,
        out_shape=[
            jax.ShapeDtypeStruct((PAIRS, LENGTH, D), BF16),
            jax.ShapeDtypeStruct((PAIRS, LENGTH, D), BF16),
            jax.ShapeDtypeStruct((FF // 2, D), BF16),
            jax.ShapeDtypeStruct((HALF, FF), BF16),
            jax.ShapeDtypeStruct((HALF, FF), BF16),
            jax.ShapeDtypeStruct((36, 1, 128), F32),
        ],
        in_specs=[pl.BlockSpec(memory_space=pltpu.SMEM)] + [any_] * 7,
        out_specs=[any_] * 5 + [inside],
        scratch_shapes=[
            vm((PAIRS, LENGTH, D), BF16),
            vm((PAIRS, LENGTH, D), BF16),
            vm((ROWS, D), F32),
            vm((ROWS, D), BF16),
            vm((ROWS, D), BF16),
            vm((3, D, ROWS), BF16),
            vm((ROWS, 4 * D), BF16),
            vm((ROWS, D), BF16),
            vm((ROWS, 128), F32),
            vm((ROWS, D), F32),
            vm((ROWS, FF), BF16),
            vm((ROWS, FF), BF16),
            vm((ROWS, D), F32),
            vm((13, 1, D), F32),
            vm((2, 16, HALF), BF16),
            vm((D, 3 * D), BF16),
            vm((D, D), BF16),
            vm((D, FF), BF16),
            vm((FF, D), BF16),
            vm((3, 2, HALF, 256), BF16),
            vm((3, 2, HALF, 256), BF16),
            vm((3, 2, 128, D), BF16),
            vm((3, 2, 128, D), BF16),
            vm((12, 2, HALF, 256), BF16),
            vm((12, HALF, 256), BF16),
            vm((12, HALF // 2, 256), BF16),
            vm((12, NZ - 1, HALF // 8, 256), BF16),
            vm((12, HALF // 8, 256), BF16),
            vm((6, 2, 128, D), BF16),
            vm((6, 128, D), BF16),
            vm((6, 64, D), BF16),
            vm((6, NZ - 1, 16, D), BF16),
            vm((6, 16, D), BF16),
            vm((2, 36, 1, 128), F32),
            vm((7, 2, 36, 1, 128), F32),
            dma((pieces,)),
            dma((pieces,)),
            dma((6,)),
            dma((len(SHARED), NZ - 1, 2)),
            dma((4,)),
            dma((7,)),
            dma((6,)),
            dma((6,)),
            dma((NCH,)),
            dma((2 * NP,)),
            dma((NP,)),
            dma((NP,)),
            dma((NP,)),
            dma((NP,)),
            dma((1,)),
            dma((NP,)),
            dma((2, 7)),
        ],
        compiler_params=pltpu.CompilerParams(
            collective_id=1, has_side_effects=True, vmem_limit_bytes=63 << 20
        ),
        name="layer",
    )(*arrays)


def finish_kernel(gdown, gup, gqo, gsmall, res, gtok, down, up, qkv, out, res_out, gtok_out, *vectors):
    down[...] = gdown[...].astype(F32)
    up[...] = gup[...].astype(F32)
    qkv[...] = gqo[:, : 3 * D].astype(F32)
    out[...] = gqo[:, 3 * D :].astype(F32)

    @pl.when(pl.program_id(0) == 0)
    def _():
        res_out[...] = res[...]
        gtok_out[...] = gtok[...]
        at = 0
        for v in vectors:
            n = v.shape[0] // 128
            for j in range(n):
                v[j * 128 : (j + 1) * 128] = gsmall[at + j, 0]
            at += n


def finish(gdown, gup, gqo, gsmall, res, gtok):
    steps = 3
    rows = PAIRS * LENGTH

    def cut(n, width):
        return pl.BlockSpec((n, width), lambda i: (i, 0))

    tokens = pl.BlockSpec((rows, D), lambda i: (0, 0))
    out = pl.pallas_call(
        finish_kernel,
        grid=(steps,),
        out_shape=[
            jax.ShapeDtypeStruct((FF // 2, D), F32),
            jax.ShapeDtypeStruct((HALF, FF), F32),
            jax.ShapeDtypeStruct((HALF, 3 * D), F32),
            jax.ShapeDtypeStruct((HALF, D), F32),
            jax.ShapeDtypeStruct((PAIRS * LENGTH, D), BF16),
            jax.ShapeDtypeStruct((PAIRS * LENGTH, D), BF16),
        ]
        + [jax.ShapeDtypeStruct((n * HALF,), F32) for n in SMALL],
        in_specs=[
            cut(FF // 2 // steps, D),
            cut(HALF // steps, FF),
            cut(HALF // steps, FF),
            pl.BlockSpec((36, 1, 128), lambda i: (0, 0, 0)),
            tokens,
            tokens,
        ],
        out_specs=[
            cut(FF // 2 // steps, D),
            cut(HALF // steps, FF),
            cut(HALF // steps, 3 * D),
            cut(HALF // steps, D),
            tokens,
            tokens,
        ]
        + [pl.BlockSpec((n * HALF,), lambda i: (0,)) for n in SMALL],
        name="finish",
    )(gdown, gup, gqo, gsmall, res.reshape(PAIRS * LENGTH, D), gtok.reshape(PAIRS * LENGTH, D))
    return out


def on_device(extra, tokens, patch_counts, cotangent, norm1_gain, norm1_bias, qkv_weight, qv_bias,
              out_weight, out_bias, norm2_gain, norm2_bias, up_weight, up_bias, down_weight, down_bias):
    small, at = 0, 0
    for v in (norm1_gain, norm1_bias, qv_bias, out_bias, norm2_gain, norm2_bias, up_bias, down_bias):
        small = small + jnp.pad(v, (at, 16 * HALF - at - v.size))
        at += v.size
    small = small.reshape(16, HALF)
    result, grad_tokens, gdown, gup, gqo, gsmall = layer(
        patch_counts, tokens, cotangent, qkv_weight, out_weight, up_weight, down_weight, small
    )
    down, up, qkv, out, result, grad_tokens, *parts = finish(gdown, gup, gqo, gsmall, result, grad_tokens)
    grads = [down, up, qkv, out] + parts
    if extra is not None:
        grads = lax.psum(grads, "dp", axis_index_groups=extra)
    down, up, qkv, out, *parts = grads
    result, grad_tokens = (v.reshape(PAIRS, LENGTH, D) for v in (result, grad_tokens))
    return (
        result, grad_tokens, parts[0], parts[1], qkv, parts[2], out, parts[3],
        parts[4], parts[5], up, parts[6], down, parts[7],
    )


def solution(mesh):
    dp = mesh.shape["dp"]
    extra = None
    if dp > GROUP:
        extra = [[j + GROUP * i for i in range(dp // GROUP)] for j in range(GROUP)]
    row = P(("dp", "fsdp"), None, None)
    vec = P("fsdp")
    mat = P("fsdp", None)
    return jax.shard_map(
        functools.partial(on_device, extra),
        mesh=mesh,
        in_specs=(row, P(("dp", "fsdp")), row, vec, vec, mat, vec, mat, vec, vec, vec, mat, vec, mat, vec),
        out_specs=(row, row, vec, vec, mat, vec, mat, vec, vec, vec, mat, vec, mat, vec),
        check_vma=False,
    )
```

```python
import functools

import jax
import jax.numpy as jnp
from jax import lax
from jax.experimental import pallas as pl
from jax.experimental.pallas import tpu as pltpu
from jax.sharding import PartitionSpec as P

TEXT = 40
MESH = pl.DeviceIdType.MESH
BF16 = jnp.bfloat16
F32 = jnp.float32
EPS = 1e-06
NZ = 4
GROUP = 16
PAIRS = 2
LENGTH = 280
LPAD = 288
ROWS = PAIRS * LPAD
D = 768
FF = 3072
HALF = D // 2
NCH = 18
SPLIT = 18
PARTS = [(i, 0, None) for i in range(SPLIT)] + [(i, 128 * e, 128) for i in range(SPLIT, NCH) for e in range(2)]
NP = len(PARTS)
YFIRST = (1, 3, 5)
GW = 5
PIECES = (
    [(2, 4, 0, 96, FF // 2, FF // 8, 0, FF // 8)]
    + [(0, j, 0, 96, k * D + j * 256, 256, 0, 0) for j in range(3) for k in range(3)]
    + [(1, 3, 48 * j, 48, 0, D, 0, 0) for j in range(2)]
    + [(2, 4, 0, 96, 384 * j, 384, 0, 0) for j in range(4)]
    + [(3, 5, 0, 48, 0, D, 48, 0)]
    + [(3, 5, 192 + 96 * j, 96, 0, D, 0, 0) for j in range(2)]
)
SHARED = [g for g, p in enumerate(PIECES) if p[6] or p[7]]
GLAG = 3
STEPS = len(PIECES) + GLAG
SMALL = (1, 1, 2, 1, 1, 1, 4, 1)
G1, B1, QV, OB, G2, B2, UB, DB = 0, 1, 2, 4, 5, 6, 7, 11


def plan():
    points = list(POINTS)
    points += [("Z%d" % n, NCH, n + 1) for n in range(points[-1][2], SLOTS)]
    acts, done, started = {}, 0, 0
    for name, ready, upto in points:
        todo = acts[name] = []
        while True:
            ahead = AHEAD if done < NARROW else AHEAD_LAST
            while started < min(2 * NP, 2 * BY[ready], done + ahead):
                todo.append(("start", started))
                started += 1
            if done == upto:
                break
            assert done >= 2 * NP or started > done
            todo.append(("slot", done))
            done += 1
    return acts


POINTS = (
    ("A1", 1, 0), ("A2", 1, 0), ("A3", 2, 1), ("A4", 3, 2), ("A5", 4, 3), ("B", 6, 5), ("C0", 6, 6), ("C1", 6,
    8), ("C2", 7, 9), ("C3", 8, 10), ("C4", 9, 11), ("C5", 10, 13), ("D", 12, 14), ("E0", 12, 15), ("E", 13,
    17), ("F0", 13, 17), ("F1", 13, 17), ("F2", 13, 18), ("F3", 13, 18), ("F4", 13, 19), ("F5", 13, 20),
    ("F6", 13, 20), ("F7", 13, 21), ("F8", 13, 22), ("F9", 13, 22), ("F10", 13, 23), ("F11", 13, 24), ("G2",
    14, 25), ("G3", 15, 26), ("G4", 16, 26), ("H", 18, 27), ("I", 18, 29),
)
SLOTS = 2 * NP + 17
BY = [sum(p[0] < n for p in PARTS) for n in range(NCH + 1)]
AHEAD, AHEAD_LAST, NARROW = 6, 4, 24
PLAN = plan()


def dot(a, b):
    return jnp.dot(a, b, preferred_element_type=F32)


def dot_nt(a, b):
    return lax.dot_general(a, b, (((1,), (1,)), ((), ())), preferred_element_type=F32)


def dot_tn(a, b):
    return lax.dot_general(a, b, (((0,), (0,)), ((), ())), preferred_element_type=F32)


def mult(x, n):
    return x if isinstance(x, int) else pl.multiple_of(x, n)


def ds(start, size, n=None):
    return pl.ds(mult(start, n or size), size)


def places():
    d = lax.axis_index("dp")
    f = lax.axis_index("fsdp")
    core = lax.rem(d, 2)
    y = lax.rem(d // 2, 2)
    z = lax.rem(d // 4, NZ)
    base = d - lax.rem(d, GROUP)

    def at(zz, yy, cc):
        return base + zz * 4 + yy * 2 + cc

    peers = {
        "c": (at(z, y, 1 - core), f),
        "x": (d, 1 - f),
        "y": (at(z, 1 - y, core), f),
    }
    for k in range(1, NZ):
        peers["z%d" % k] = (at(lax.rem(z + k, NZ), y, core), f)
    return f, core, y, z, peers


def norm_parts(v):
    c = v - jnp.mean(v, axis=-1, keepdims=True)
    r = lax.rsqrt(jnp.mean(c * c, axis=-1, keepdims=True) + EPS)
    return c * r, r


def layer_kernel(
    counts, tok, cot, w0, w1, w2, w3, s_in,
    res, gtok, gdown, gup, gqo, gsmall,
    tokv, cotv, xs, dys, h, lt, qkv, o, lse, x1, gact, dact, dh, vec, smv,
    v0, v1, v2, v3,
    own, snd, ownd, sndd,
    cb, xb, yb, zb, stg, cbd, xbd, ybd, zbd, stgd, sacc, srecv,
    gxs, gys, gcs, gzs, gsent, lsem, csent, rsent, csem, xsem, ysem, zsem, zbsem, azsem, azasem, aysem, acsem, psem, ssem,
):
    f, core, y, z, peers = places()
    ins = (w0, w1, w2, w3)
    ws = (v0, v1, v2, v3)
    barrier = pltpu.get_barrier_semaphore()
    for name in peers:
        pl.semaphore_signal(barrier, inc=1, device_id=peers[name], device_id_type=MESH)
    met = len(peers)
    b0, b1 = lax.rem(z, 2), z // 2
    dev = lax.axis_index("dp")
    peers["p"] = (dev + 4 - 8 * b0, f)

    def send(src, dst, sent, arrived, name):
        return pltpu.make_async_remote_copy(
            src_ref=src, dst_ref=dst, send_sem=sent, recv_sem=arrived,
            device_id=peers[name], device_id_type=MESH,
        )

    def piece(g, half, yy, zz=None):
        w, _, r0, rows, c0, cols, zr, zc = PIECES[g]
        full = ins[w].shape[0]
        zz = z if zz is None else zz
        start = half * full + (core * 2 + yy) * (full // 4) + r0 + zz * zr
        return w, (pl.ds(pl.multiple_of(start, 16), rows), ds(c0 + zz * zc, cols, 128))

    def same(g, yy, zz, sent, arrived, name):
        w, at = piece(g, 1 - f, yy, zz)
        return send(ws[w].at[at], ws[w].at[at], sent, arrived, name)

    def gx(g):
        w, there = piece(g, f, y)
        _, here = piece(g, 0, y)
        return send(ins[w].at[here], ws[w].at[there], gsent.at[0], gxs.at[g], "x")

    def gy(g):
        return same(g, y, z, gsent.at[1], gys.at[g], "y")

    def gc(g, e, k=0):
        arrived = gcs.at[PIECES[g][1]]
        return same(g, y if e == 0 else 1 - y, lax.rem(z + NZ - k, NZ), gsent.at[2], arrived, "c")

    def gz(g, e, k):
        return same(g, y if e == 0 else 1 - y, z, gsent.at[3], gzs.at[SHARED.index(g), k - 1, e], "z%d" % k)

    def got_x(g):
        gx(g).wait_recv()
        if g + GW < len(PIECES):
            gx(g + GW).start()
        gy(g).start()
        gc(g, 0).start()
        if g in SHARED:
            for k in range(1, NZ):
                gz(g, 0, k).start()

    def got_y(g):
        gy(g).wait_recv()
        gc(g, 1).start()
        if g in SHARED:
            for k in range(1, NZ):
                gz(g, 1, k).start()

    def step(n):
        if n < len(PIECES):
            got_x(n)
        if n >= GLAG:
            got_y(n - GLAG)

    def steps(first, last):
        for n in range(first, last + 1):
            step(n)

    def got_z(g, k):
        for e in range(2):
            gz(g, e, k).wait_recv()
            gc(g, e, k).start()

    def whole(sem, rows):
        at = v3.at[pl.ds(0, rows)]
        return send(at, at, sem, sem, "c")

    def got(j):
        whole(gcs.at[j], (192, 192, 192, 192, 768, 768)[j]).wait_recv()

    rows_in = (pltpu.make_async_copy(tok, tokv, lsem.at[5]), pltpu.make_async_copy(cot, cotv, lsem.at[6]))
    rows_in[0].start()
    local = []
    for i in range(4):
        full = ins[i].shape[0]
        local.append(pltpu.make_async_copy(ins[i], ws[i].at[pl.ds(pl.multiple_of(f * full, 16), full)], lsem.at[i]))
    local.append(pltpu.make_async_copy(s_in, smv.at[f], lsem.at[4]))
    local[4].start()
    pl.semaphore_wait(barrier, met)
    small_x = send(s_in, smv.at[f], ssem.at[0, 6], ssem.at[1, 6], "x")
    small_x.start()
    for g in range(GW):
        gx(g).start()
    rows_in[1].start()
    for i in range(4):
        local[i].start()

    def c_copy(i, down):
        if down:
            return send(sndd.at[lax.rem(i, 3)], cbd.at[i], csent.at[lax.rem(i, 3)], csem.at[i], "c")
        return send(snd.at[lax.rem(i, 3)], cb.at[i - 6], csent.at[3 + lax.rem(i, 3)], csem.at[i], "c")

    def bufs(i):
        if i < 6:
            return i, 128, D, cbd, xbd, ybd, zbd, stgd
        return i - 6, HALF, 256, cb, xb, yb, zb, stg

    def bufs(n):
        i, c0, width = PARTS[n]
        if i < 6:
            j, ur, refs = i, 128, (cbd, xbd, ybd, zbd, stgd)
        else:
            j, ur, refs = i - 6, HALF, (cb, xb, yb, zb, stg)
        if width is None:
            return (ur,) + tuple(r.at[j] for r in refs)
        at = pl.ds(c0, width)
        cc, xx, yy, zz, st = refs
        return ur, cc.at[j, :, :, at], xx.at[j, :, at], yy.at[j, :, at], zz.at[j, :, :, at], st.at[j, :, at]

    def first_hop(n, e):
        ur = bufs(n)[0]
        if n in YFIRST:
            g = 1 - f if e == 0 else f
            return (g, ds((1 - y) * (ur // 2), ur // 2)), ds(g * (ur // 2), ur // 2), (g, ds(y * (ur // 2), ur // 2))
        half = ds(((1 - y) if e == 0 else y) * (ur // 2), ur // 2)
        return (1 - f, half), half, (f, half)

    def x_copy(h):
        n, e = h // 2, h % 2
        _, cc, xx, _, _, _ = bufs(n)
        there, here, _ = first_hop(n, e)
        return send(cc.at[there], xx.at[here], rsent.at[0], xsem.at[h], "y" if n in YFIRST else "x")

    def y_copy(n):
        _, _, xx, yy, _, _ = bufs(n)
        return send(xx.at[first_hop(n, 0)[1]], yy, rsent.at[1], ysem.at[n], "x" if n in YFIRST else "y")

    def za_copy(n, m):
        ur, _, _, yy, zz, _ = bufs(n)
        src = yy.at[ds((1 - b0) * (ur // 4) + m * (ur // 8), ur // 8, 16)]
        return send(src, zz.at[m], rsent.at[2], zsem.at[n], "p")

    def zb_copy(n):
        ur, _, _, yy, zz, _ = bufs(n)
        src = yy.at[ds(b0 * (ur // 4) + (1 - b1) * (ur // 8), ur // 8, 16)]
        return send(src, zz.at[2], rsent.at[2], zbsem.at[n], "z2")

    def outpart(n, start, rows):
        i, c0, width = PARTS[n]
        j = i % 6 if i < 12 else (i - 12 + 5) % 6
        if i < 6:
            return gdown.at[pl.ds(pl.multiple_of((2 * j + core) * 128 + start, 16), rows), :]
        ref = gup if i < 12 else gqo
        return ref.at[pl.ds(mult(start, 16), rows), ds((2 * j + core) * 256 + c0, width or 256, 128)]

    def own_piece(n):
        ur, _, _, _, _, st = bufs(n)
        return outpart(n, y * (ur // 2) + b0 * (ur // 4) + b1 * (ur // 8), ur // 8), st

    def p_copy(n):
        dst, src = own_piece(n)
        return pltpu.make_async_copy(src, dst, psem.at[n])

    def azb_copy(n):
        dst, src = own_piece(n)
        return send(src, dst, rsent.at[3], azsem.at[n], "z2")

    def aza_copy(n):
        ur = bufs(n)[0]
        part = outpart(n, y * (ur // 2) + b0 * (ur // 4), ur // 4)
        return send(part, part, rsent.at[3], azasem.at[n], "p")

    def ay_copy(n):
        ur = bufs(n)[0]
        part = outpart(n, y * (ur // 2), ur // 2)
        return send(part, part, rsent.at[4], aysem.at[n], "y")

    def ac_copy(n):
        part = outpart(n, 0, bufs(n)[0])
        return send(part, part, rsent.at[5], acsem.at[0], "c")

    def s1(i, down):
        c_copy(i, down).wait()
        if down:
            cbd[i] = (cbd[i].astype(F32) + ownd[lax.rem(i, 3)].astype(F32)).astype(BF16)
        else:
            cb[i - 6] = (cb[i - 6].astype(F32) + own[lax.rem(i, 3)].astype(F32)).astype(BF16)

    def s2(h):
        x_copy(h).wait_recv()
        n = h // 2
        if h % 2 == 0:
            _, cc, xx, _, _, _ = bufs(n)
            _, here, kept = first_hop(n, 0)
            xx[here] = (xx[here].astype(F32) + cc[kept].astype(F32)).astype(BF16)
            y_copy(n).start()

    def s3(n):
        y_copy(n).wait_recv()
        _, cc, xx, yy, _, _ = bufs(n)
        _, here, kept = first_hop(n, 1)
        yy[...] = (yy[...].astype(F32) + (xx[here].astype(F32) + cc[kept].astype(F32))).astype(BF16)
        for m in range(2):
            za_copy(n, m).start()

    def s3b(n):
        ur, _, _, yy, zz, _ = bufs(n)
        two = zz.at[pl.ds(0, 2)]
        send(two, two, rsent.at[2], zsem.at[n], "p").wait_recv()
        for m in range(2):
            at = ds(b0 * (ur // 4) + m * (ur // 8), ur // 8, 16)
            yy[at] = (yy[at].astype(F32) + zz[m].astype(F32)).astype(BF16)
        zb_copy(n).start()

    def s4(n):
        ur, _, _, yy, zz, st = bufs(n)
        zb_copy(n).wait_recv()
        at = ds(b0 * (ur // 4) + b1 * (ur // 8), ur // 8, 16)
        st[...] = (yy[at].astype(F32) + zz[2].astype(F32)).astype(BF16)
        p_copy(n).start()
        azb_copy(n).start()

    def s5a(n):
        p_copy(n).wait()
        azb_copy(n).wait_recv()
        aza_copy(n).start()

    def s5(n):
        aza_copy(n).wait_recv()
        ay_copy(n).start()

    def s6(n):
        ay_copy(n).wait_recv()
        ac_copy(n).start()

    def slot(n):
        if n < 2 * NP:
            s2(n)
        for lag, stage in ((3, s3), (6, s3b), (9, s4), (12, s5a), (15, s5), (18, s6)):
            if (n - lag) % 2 == 0 and 0 <= (n - lag) // 2 < NP:
                stage((n - lag) // 2)

    def point(name):
        for what, n in PLAN[name]:
            if what == "start":
                x_copy(n).start()
            else:
                slot(n)

    rows_in[0].wait()
    for p in range(PAIRS):
        xs[p * LPAD : p * LPAD + LENGTH] = tokv[p].astype(F32)
        xs[p * LPAD + LENGTH : (p + 1) * LPAD] = jnp.zeros((LPAD - LENGTH, D), F32)

    local[4].wait()
    small_x.wait()
    s0 = smv[0].astype(F32)
    s1v = smv[1].astype(F32)
    for j, r in enumerate((G1, B1, OB, G2, B2, DB)):
        vec[j] = jnp.concatenate([s0[r : r + 1], s1v[r : r + 1]], axis=1)
    vec[6] = jnp.concatenate([s0[QV : QV + 1], s0[QV + 1 : QV + 2]], axis=1)
    vec[7] = jnp.zeros((1, D), F32)
    vec[8] = jnp.concatenate([s1v[QV : QV + 1], s1v[QV + 1 : QV + 2]], axis=1)
    vec[9] = jnp.concatenate([s0[UB : UB + 1], s0[UB + 1 : UB + 2]], axis=1)
    vec[10] = jnp.concatenate([s0[UB + 2 : UB + 3], s0[UB + 3 : UB + 4]], axis=1)
    vec[11] = jnp.concatenate([s1v[UB : UB + 1], s1v[UB + 1 : UB + 2]], axis=1)
    vec[12] = jnp.concatenate([s1v[UB + 2 : UB + 3], s1v[UB + 3 : UB + 4]], axis=1)

    def loop(n, body):
        def step(i, carry):
            body(i)
            return carry

        lax.fori_loop(0, n, step, 0)

    def transpose_into(src, k):
        def body(j):
            cols = ds(j * 128, 128)
            lt[k, cols, :] = src[:, cols].astype(F32).T.astype(BF16)

        loop(D // 128, body)

    def ln1(i):
        rows = ds(i * 96, 96)
        n, _ = norm_parts(xs[rows])
        h[rows] = (n * vec[0] + vec[1]).astype(BF16)

    loop(6, ln1)
    steps(0, 1)
    transpose_into(h, 0)
    steps(2, 3)
    rows_in[1].wait()
    for p in range(PAIRS):
        dys[p * LPAD : (p + 1) * LPAD] = jnp.concatenate(
            [cotv[p].astype(F32), jnp.zeros((LPAD - LENGTH, D), F32)], axis=0
        ).astype(BF16)
    steps(4, 6)

    def qkv_body(j, i):
        cols = ds(i * D + j * 256, 256)
        qkv[:, cols] = (dot(h[...], v0[:, cols]) + vec[6 + i, :, j * 256 : (j + 1) * 256]).astype(BF16)

    lane = lax.broadcasted_iota(jnp.int32, (1, 128), 1)
    low = lane < 64
    key = lax.broadcasted_iota(jnp.int32, (1, LPAD), 1)

    def attend(p, hp):
        rows = ds(p * LPAD, LPAD)
        q = qkv[rows, ds(hp * 128, 128)].astype(F32) * 0.125
        k = qkv[rows, ds(D + hp * 128, 128)]
        v = qkv[rows, ds(2 * D + hp * 128, 128)]
        valid = key < TEXT + counts[p]
        outs = []
        ls = lse[rows]
        for e in range(2):
            qm = jnp.where(low if e == 0 else jnp.logical_not(low), q, 0.0).astype(BF16)
            s = jnp.where(valid, dot_nt(qm, k), -1e30)
            m = jnp.max(s, axis=-1, keepdims=True)
            ex = jnp.exp(s - m)
            t = jnp.sum(ex, axis=-1, keepdims=True)
            ls = jnp.where(lane == 2 * hp + e, m + jnp.log(t), ls)
            outs.append(dot((ex * (1.0 / t)).astype(BF16), v))
        lse[rows] = ls
        o[rows, ds(hp * 128, 128)] = jnp.where(low, outs[0], outs[1]).astype(BF16)

    local[0].wait()
    for j in range(3):
        if j:
            step(6 + 3 * j)
        got(j)
        for i in range(3):
            qkv_body(j, i)

        def heads(i):
            for n in range(2):
                pl.when(i == n)(functools.partial(step, 7 + 3 * j + n))
            for p in range(PAIRS):
                attend(p, 2 * j + i)

        loop(2, heads)
    step(15)
    got(3)
    local[1].wait()

    def proj(i):
        cols = ds(i * 256, 256)
        x1[:, cols] = xs[:, cols] + dot(o[...], v1[:, cols]) + vec[2, :, cols]

    loop(3, proj)
    steps(16, 17)

    def ln2(i):
        rows = ds(i * 96, 96)
        n, _ = norm_parts(x1[rows])
        h[rows] = (n * vec[3] + vec[4]).astype(BF16)

    loop(6, ln2)
    step(18)
    for k in range(1, NZ):
        got_z(SHARED[0], k)
    got(4)
    local[2].wait()

    def up_tile(j):
        cols = ds(j * 256, 256)
        u = dot(h[...], v2[:, cols]) + vec[9 + j // 3, :, ds(lax.rem(j, 3) * 256, 256)]
        phi = 0.5 * (1.0 + lax.erf(u * 0.7071067811865476))
        gact[:, cols] = (u * phi).astype(BF16)
        dact[:, cols] = (phi + u * (0.3989422804014327 * jnp.exp(-0.5 * u * u))).astype(BF16)

    def down_chunk(i):
        par = lax.rem(i, 3)
        for x in range(2):
            cols = x * (FF // 2) + i * 256
            mine = gact[:, ds(cols + core * 128, 128)]
            other = gact[:, ds(cols + (1 - core) * 128, 128)]
            both = jnp.concatenate([mine, other], axis=1)
            for n in range(3):
                r = dot_tn(both, dys[:, n * 256 : (n + 1) * 256]).astype(BF16)
                ownd[par, x, :, n * 256 : (n + 1) * 256] = r[:128]
                sndd[par, x, :, n * 256 : (n + 1) * 256] = r[128:]
        c_copy(i, True).start()

    def phase_a(i):
        up_tile(i)
        for when, ns in ((0, (19,)), (1, (20, 21)), (2, (22,))):
            if ns[0] < STEPS:
                pl.when(i == when)(functools.partial(steps, ns[0], min(ns[-1], STEPS - 1)))
        for k in range(1, NZ):
            pl.when(i == k + 2)(functools.partial(got_z, SHARED[1], k))
        up_tile(6 + i)

        @pl.when(i == 1)
        def _():
            s1(0, True)

        @pl.when(i > 2)
        def _():
            s1(i - 2, True)

        for when in range(1, 6):
            pl.when(i == when)(functools.partial(point, "A%d" % when))
        down_chunk(i)

    loop(6, phase_a)
    transpose_into(o, 1)
    transpose_into(h, 2)
    got(5)
    local[3].wait()

    def down_proj(n):
        cols = ds(n * 256, 256)
        r = (x1[:, cols] + dot(gact[...], v3[:, cols]) + vec[5, :, cols])
        for p in range(PAIRS):
            tokv[p, :, cols] = r[p * LPAD : p * LPAD + LENGTH].astype(BF16)

    loop(3, down_proj)
    result_out = pltpu.make_async_copy(tokv, res, lsem.at[5])
    result_out.start()
    s1(4, True)
    s1(5, True)
    point("B")

    def du_tile(j):
        cols = ds(j * 256, 256)
        du = (dot_nt(dys[...], v3[cols, :]) * dact[:, cols].astype(F32)).astype(BF16)
        dact[:, cols] = du
        sums = jnp.sum(du.astype(F32), axis=0, keepdims=True)
        for e in range(2):
            sacc[j // 6, 3 * UB + 2 * lax.rem(j, 6) + e] = sums[:, e * 128 : (e + 1) * 128]

    def col_chunk(i, j, sel, src):
        par = lax.rem(i, 3)
        for side, dst in ((core, own), (1 - core, snd)):
            u = 2 * j + side
            col_unit(dst, par, u, sel, src)
        c_copy(i, False).start()

    def col_unit(dst, par, u, sel, src):
        r = dot(lt[sel], src[:, ds(u * 256, 256)]).astype(BF16)
        dst[par, 0] = r[:HALF]
        dst[par, 1] = r[HALF:]

    def phase_c(j):
        du_tile(2 * j)
        du_tile(2 * j + 1)

        @pl.when(j > 1)
        def _():
            s1(4 + j, False)

        for when in range(6):
            pl.when(j == when)(functools.partial(point, "C%d" % when))
        col_chunk(6 + j, j, 2, dact)

    loop(6, phase_c)

    def dh2_tile(n):
        cols = ds(n * 256, 256)
        dh[:, cols] = dot_nt(dact[...], v2[cols, :])

    loop(3, dh2_tile)
    s1(10, False)
    s1(11, False)
    point("D")
    zero = jnp.zeros((1, D), F32)

    def spread(x, r, v):
        for j in range(v.shape[1] // 128):
            sacc[x, 3 * r + j] = v[:, j * 128 : (j + 1) * 128]

    def put(r, v):
        spread(0, r, v[:, :HALF])
        spread(1, r, v[:, HALF:])

    def ln2_back(i, carry):
        a, b, c2, d2 = carry
        rows = ds(i * 96, 96)
        n, r = norm_parts(x1[rows])
        g = dh[rows]
        e = g * vec[3]
        dy = dys[rows].astype(F32)
        dx = dy + r * (
            e - jnp.mean(e, axis=-1, keepdims=True) - n * jnp.mean(e * n, axis=-1, keepdims=True)
        )
        x1[rows] = dx
        da = dx.astype(BF16)
        qkv[rows, 3 * D :] = da
        return (
            a + jnp.sum(g * n, axis=0, keepdims=True),
            b + jnp.sum(g, axis=0, keepdims=True),
            c2 + jnp.sum(da.astype(F32), axis=0, keepdims=True),
            d2 + jnp.sum(dy, axis=0, keepdims=True),
        )

    sums = lax.fori_loop(0, 6, ln2_back, (zero, zero, zero, zero))
    for r, v in zip((G2, B2, OB, DB), sums):
        put(r, v)

    col_chunk(12, 5 + core // 2, 1, qkv)

    point("E0")

    def do_tile(n):
        cols = ds(n * 256, 256)
        o[:, cols] = dot_nt(qkv[:, 3 * D :], v1[cols, :]).astype(BF16)

    loop(3, do_tile)
    s1(12, False)
    point("E")

    def attend_back(p, hp):
        rows = ds(p * LPAD, LPAD)
        q = qkv[rows, ds(hp * 128, 128)]
        k = qkv[rows, ds(D + hp * 128, 128)]
        v = qkv[rows, ds(2 * D + hp * 128, 128)]
        g = o[rows, ds(hp * 128, 128)]
        qf = q.astype(F32) * 0.125
        gf = g.astype(F32)
        valid = key < TEXT + counts[p]
        ls = lse[rows]
        got3 = []
        for e in range(2):
            keep = low if e == 0 else jnp.logical_not(low)
            qm = jnp.where(keep, qf, 0.0).astype(BF16)
            gm = jnp.where(keep, gf, 0.0).astype(BF16)
            total = jnp.sum(jnp.where(lane == 2 * hp + e, ls, 0.0), axis=-1, keepdims=True)
            pr = jnp.where(valid, jnp.exp(dot_nt(qm, k) - total), 0.0)
            dp = dot_nt(gm, v)
            dsc = (pr * (dp - jnp.sum(pr * dp, axis=-1, keepdims=True))).astype(BF16)
            got3.append((dot(dsc, k), dot_tn(dsc, q), dot_tn(pr.astype(BF16), g)))
        for part, scale in ((0, 0.125), (1, 0.125), (2, 1.0)):
            r = jnp.where(low, got3[0][part], got3[1][part]) * scale
            qkv[rows, ds(part * D + hp * 128, 128)] = r.astype(BF16)

    def heads_back(i):
        for when in range(6):
            pl.when(i == when)(lambda when=when: [point("F%d" % (2 * when + e)) for e in range(2)] and None)
        for p in range(PAIRS):
            attend_back(p, i)

    loop(6, heads_back)

    def phase_g(t):
        @pl.when(t > 1)
        def _():
            s1(11 + t, False)

        for when in range(2, 4):
            pl.when(t == when)(functools.partial(point, "G%d" % when))
        col_chunk(13 + t, t, 0, qkv)

    loop(4, phase_g)
    for c in range(2):

        @pl.when(core == c)
        def _():
            for side, dst in ((c, own), (1 - c, snd)):
                col_unit(dst, 17 % 3, 8 + side, side, qkv)

    c_copy(17, False).start()
    s1(15, False)
    point("G4")

    def dh1_tile(n):
        cols = ds(n * 256, 256)
        dh[:, cols] = dot_nt(qkv[:, : 3 * D], v0[cols, :])

    loop(3, dh1_tile)
    s1(16, False)
    s1(17, False)
    point("H")

    def ln1_back(i, carry):
        a, b, qs, vs = carry
        rows = ds(i * 96, 96)
        n, r = norm_parts(xs[rows])
        g = dh[rows]
        e = g * vec[0]
        xs[rows] = x1[rows] + r * (
            e - jnp.mean(e, axis=-1, keepdims=True) - n * jnp.mean(e * n, axis=-1, keepdims=True)
        )
        return (
            a + jnp.sum(g * n, axis=0, keepdims=True),
            b + jnp.sum(g, axis=0, keepdims=True),
            qs + jnp.sum(qkv[rows, :D].astype(F32), axis=0, keepdims=True),
            vs + jnp.sum(qkv[rows, 2 * D : 3 * D].astype(F32), axis=0, keepdims=True),
        )

    ga, gb, qs, vs = lax.fori_loop(0, 6, ln1_back, (zero, zero, zero, zero))
    put(G1, ga)
    put(B1, gb)
    for x, v in ((0, qs), (1, vs)):
        spread(x, QV, v)
    for p in range(PAIRS):
        cotv[p] = xs[p * LPAD : p * LPAD + LENGTH].astype(BF16)
    grad_out = pltpu.make_async_copy(cotv, gtok, lsem.at[6])
    grad_out.start()
    point("I")

    n = POINTS[-1][2]
    for j, name in enumerate(("c", "x", "y")):
        cp = send(sacc, srecv.at[j], ssem.at[0, j], ssem.at[1, j], name)
        cp.start()
        for _ in range(2):
            point("Z%d" % n)
            n += 1
        cp.wait()
        sacc[...] = sacc[...] + srecv[j]
    copies = [
        send(sacc, srecv.at[3 + z], ssem.at[0, 2 + k], ssem.at[1, 2 + k], "z%d" % k) for k in range(1, NZ)
    ]
    for cp in copies:
        cp.start()
    srecv[3 + z] = sacc[...]
    for _ in range(2):
        point("Z%d" % n)
        n += 1
    for cp in copies:
        cp.wait()
    gsmall[...] = (srecv[3, f] + srecv[4, f]) + (srecv[5, f] + srecv[6, f])
    while n < SLOTS:
        point("Z%d" % n)
        n += 1
    result_out.wait()
    grad_out.wait()
    whole(acsem.at[0], 2304).wait_recv()
    for sem, rows in ((0, 864), (1, 864), (2, 2304), (3, 576)):
        whole(gsent.at[sem], rows).wait_send()
    for sem, rows in ((0, 2304), (1, 1152), (2, 864), (3, 864), (4, 1152), (5, 2304)):
        whole(rsent.at[sem], rows).wait_send()


def layer(*arrays):
    vm = pltpu.VMEM
    dma = pltpu.SemaphoreType.DMA
    any_ = pl.BlockSpec(memory_space=pl.ANY)
    inside = pl.BlockSpec(memory_space=pltpu.VMEM)
    pieces = len(PIECES)
    return pl.pallas_call(
        layer_kernel,
        out_shape=[
            jax.ShapeDtypeStruct((PAIRS, LENGTH, D), BF16),
            jax.ShapeDtypeStruct((PAIRS, LENGTH, D), BF16),
            jax.ShapeDtypeStruct((FF // 2, D), BF16),
            jax.ShapeDtypeStruct((HALF, FF), BF16),
            jax.ShapeDtypeStruct((HALF, FF), BF16),
            jax.ShapeDtypeStruct((36, 1, 128), F32),
        ],
        in_specs=[pl.BlockSpec(memory_space=pltpu.SMEM)] + [any_] * 7,
        out_specs=[any_] * 5 + [inside],
        scratch_shapes=[
            vm((PAIRS, LENGTH, D), BF16),
            vm((PAIRS, LENGTH, D), BF16),
            vm((ROWS, D), F32),
            vm((ROWS, D), BF16),
            vm((ROWS, D), BF16),
            vm((3, D, ROWS), BF16),
            vm((ROWS, 4 * D), BF16),
            vm((ROWS, D), BF16),
            vm((ROWS, 128), F32),
            vm((ROWS, D), F32),
            vm((ROWS, FF), BF16),
            vm((ROWS, FF), BF16),
            vm((ROWS, D), F32),
            vm((13, 1, D), F32),
            vm((2, 16, HALF), BF16),
            vm((D, 3 * D), BF16),
            vm((D, D), BF16),
            vm((D, FF), BF16),
            vm((FF, D), BF16),
            vm((3, 2, HALF, 256), BF16),
            vm((3, 2, HALF, 256), BF16),
            vm((3, 2, 128, D), BF16),
            vm((3, 2, 128, D), BF16),
            vm((12, 2, HALF, 256), BF16),
            vm((12, HALF, 256), BF16),
            vm((12, HALF // 2, 256), BF16),
            vm((12, NZ - 1, HALF // 8, 256), BF16),
            vm((12, HALF // 8, 256), BF16),
            vm((6, 2, 128, D), BF16),
            vm((6, 128, D), BF16),
            vm((6, 64, D), BF16),
            vm((6, NZ - 1, 16, D), BF16),
            vm((6, 16, D), BF16),
            vm((2, 36, 1, 128), F32),
            vm((7, 2, 36, 1, 128), F32),
            dma((pieces,)),
            dma((pieces,)),
            dma((6,)),
            dma((len(SHARED), NZ - 1, 2)),
            dma((4,)),
            dma((7,)),
            dma((6,)),
            dma((6,)),
            dma((NCH,)),
            dma((2 * NP,)),
            dma((NP,)),
            dma((NP,)),
            dma((NP,)),
            dma((NP,)),
            dma((NP,)),
            dma((NP,)),
            dma((1,)),
            dma((NP,)),
            dma((2, 7)),
        ],
        compiler_params=pltpu.CompilerParams(
            collective_id=1, has_side_effects=True, vmem_limit_bytes=63 << 20
        ),
        name="layer",
    )(*arrays)


def finish_kernel(gdown, gup, gqo, gsmall, res, gtok, down, up, qkv, out, res_out, gtok_out, *vectors):
    down[...] = gdown[...].astype(F32)
    up[...] = gup[...].astype(F32)
    qkv[...] = gqo[:, : 3 * D].astype(F32)
    out[...] = gqo[:, 3 * D :].astype(F32)

    @pl.when(pl.program_id(0) == 0)
    def _():
        res_out[...] = res[...]
        gtok_out[...] = gtok[...]
        at = 0
        for v in vectors:
            n = v.shape[0] // 128
            for j in range(n):
                v[j * 128 : (j + 1) * 128] = gsmall[at + j, 0]
            at += n


def finish(gdown, gup, gqo, gsmall, res, gtok):
    steps = 3
    rows = PAIRS * LENGTH

    def cut(n, width):
        return pl.BlockSpec((n, width), lambda i: (i, 0))

    tokens = pl.BlockSpec((rows, D), lambda i: (0, 0))
    out = pl.pallas_call(
        finish_kernel,
        grid=(steps,),
        out_shape=[
            jax.ShapeDtypeStruct((FF // 2, D), F32),
            jax.ShapeDtypeStruct((HALF, FF), F32),
            jax.ShapeDtypeStruct((HALF, 3 * D), F32),
            jax.ShapeDtypeStruct((HALF, D), F32),
            jax.ShapeDtypeStruct((PAIRS * LENGTH, D), BF16),
            jax.ShapeDtypeStruct((PAIRS * LENGTH, D), BF16),
        ]
        + [jax.ShapeDtypeStruct((n * HALF,), F32) for n in SMALL],
        in_specs=[
            cut(FF // 2 // steps, D),
            cut(HALF // steps, FF),
            cut(HALF // steps, FF),
            pl.BlockSpec((36, 1, 128), lambda i: (0, 0, 0)),
            tokens,
            tokens,
        ],
        out_specs=[
            cut(FF // 2 // steps, D),
            cut(HALF // steps, FF),
            cut(HALF // steps, 3 * D),
            cut(HALF // steps, D),
            tokens,
            tokens,
        ]
        + [pl.BlockSpec((n * HALF,), lambda i: (0,)) for n in SMALL],
        name="finish",
    )(gdown, gup, gqo, gsmall, res.reshape(PAIRS * LENGTH, D), gtok.reshape(PAIRS * LENGTH, D))
    return out


def on_device(extra, tokens, patch_counts, cotangent, norm1_gain, norm1_bias, qkv_weight, qv_bias,
              out_weight, out_bias, norm2_gain, norm2_bias, up_weight, up_bias, down_weight, down_bias):
    small, at = 0, 0
    for v in (norm1_gain, norm1_bias, qv_bias, out_bias, norm2_gain, norm2_bias, up_bias, down_bias):
        small = small + jnp.pad(v, (at, 16 * HALF - at - v.size))
        at += v.size
    small = small.reshape(16, HALF)
    result, grad_tokens, gdown, gup, gqo, gsmall = layer(
        patch_counts, tokens, cotangent, qkv_weight, out_weight, up_weight, down_weight, small
    )
    down, up, qkv, out, result, grad_tokens, *parts = finish(gdown, gup, gqo, gsmall, result, grad_tokens)
    grads = [down, up, qkv, out] + parts
    if extra is not None:
        grads = lax.psum(grads, "dp", axis_index_groups=extra)
    down, up, qkv, out, *parts = grads
    result, grad_tokens = (v.reshape(PAIRS, LENGTH, D) for v in (result, grad_tokens))
    return (
        result, grad_tokens, parts[0], parts[1], qkv, parts[2], out, parts[3],
        parts[4], parts[5], up, parts[6], down, parts[7],
    )


def solution(mesh):
    dp = mesh.shape["dp"]
    extra = None
    if dp > GROUP:
        extra = [[j + GROUP * i for i in range(dp // GROUP)] for j in range(GROUP)]
    row = P(("dp", "fsdp"), None, None)
    vec = P("fsdp")
    mat = P("fsdp", None)
    return jax.shard_map(
        functools.partial(on_device, extra),
        mesh=mesh,
        in_specs=(row, P(("dp", "fsdp")), row, vec, vec, mat, vec, mat, vec, vec, vec, mat, vec, mat, vec),
        out_specs=(row, row, vec, vec, mat, vec, mat, vec, vec, vec, mat, vec, mat, vec),
        check_vma=False,
    )
```
